32 devices in a mesh: dp: 8 (over z, y), expert: 4 (over x, core).
Axes of the slice: x: 2, y: 2, z: 4, core: 2. Of those that a mesh axis runs over, the one named last changes fastest.
Arguments:
- master_old: float32 [8, 4, 16, 128], P('dp', 'expert'), may hold values from -1.5 to 1.5
- m_codes: bfloat16 [8, 4, 16, 128], P('dp', 'expert'), may hold values from -1 to 1
- m_scale: float32 [8, 4, 16], P('dp', 'expert'), may hold values from 0.05 to 0.5
- v_codes: bfloat16 [8, 4, 16, 128], P('dp', 'expert'), may hold values from 0.049804688 to 1
- v_scale: float32 [8, 4, 16], P('dp', 'expert'), may hold values from 0.1 to 1
- grad_parts: bfloat16 [8, 4, 128, 128], P('dp', 'expert'), may hold values from -100 to 100, as said below
- send_order: int32 [8, 4, 16], P('dp', 'expert'), may hold values from 0 to 15, each once within a row
- recv_place: int32 [8, 4, 16], P('dp', 'expert'), may hold values from 0 to 15, each once within a row
Outputs:
- master_new: float32 [4, 128, 128], P('expert', 'dp')
- m_codes_new: bfloat16 [4, 128, 128], P('expert', 'dp')
- m_scale_new: float32 [4, 128], P('expert', 'dp')
- v_codes_new: bfloat16 [4, 128, 128], P('expert', 'dp')
- v_scale_new: float32 [4, 128], P('expert', 'dp')
The draws below stay inside these ranges and needn't reach their ends.
Inputs may be any that keep to these rules, and one draw needn't show every extreme that they name: `grad_parts`: partial gradients of one data shard.
All inputs are finite; a program needn't handle non-finite values. Where the reference program divides by a largest or mean magnitude, that divisor is 1e-20 or more.
Results may differ from the reference program's by a relative error of at most 0.0004.
Values may be sent and summed in bfloat16 or wider, within the bound.
A program may use at most 64 MiB of HBM per device.

```python
import math
import jax
import jax.numpy as jnp
from jax import lax

BLOCK = 128
BLK_DEV = 16
STEP = 200
SHARD_TOTAL = 8
GROUPS = 4
GROUP_BLK = 128


def draw_grad_parts(key, part):
    key_base = jax.random.fold_in(key, 11)
    key_pair = jax.random.fold_in(key, 12)
    key_common = jax.random.fold_in(key, 13)
    key_group = jax.random.fold_in(key, 14)
    key_share = jax.random.fold_in(key, 15)
    key_rows = jax.random.fold_in(key, 16)
    spike_key = jax.random.fold_in(key, 17)
    shape_all = (SHARD_TOTAL, GROUPS, GROUP_BLK, BLOCK)
    values = jax.random.normal(key_base, shape_all, jnp.float32)
    steepness = 2.0
    row_logarithm = jax.random.uniform(key_rows, (SHARD_TOTAL,), jnp.float32, -1.5, 1.5)
    spike_factor = 2.0
    common = jax.random.normal(key_common, (1, GROUPS, GROUP_BLK, BLOCK), jnp.float32)
    group_scale = jnp.exp(jax.random.uniform(key_group, (GROUPS,), jnp.float32, 0.0, math.log(4.0)))
    group_share = jnp.exp(jax.random.uniform(key_share, (GROUPS,), jnp.float32, math.log(0.25), math.log(4.0)))
    spike_row = jax.random.randint(spike_key, (), 0, SHARD_TOTAL)
    row_position_index = jnp.arange(SHARD_TOTAL)
    row_surplus = jnp.where(row_position_index == spike_row, spike_factor * SHARD_TOTAL, jnp.exp(row_logarithm * math.log(10.0)))
    excess = group_share[:, None] * row_surplus[None, :]
    common_weight = jnp.sqrt(excess / SHARD_TOTAL)
    shard_of = jnp.arange(GROUP_BLK) // BLK_DEV
    weight_rows = common_weight[:, shard_of]
    values = values + weight_rows[None, :, :, None] * common
    rising = 1.0 + steepness * shard_of.astype(jnp.float32) / max(SHARD_TOTAL - 1, 1)
    paired = jax.random.permutation(key_pair, SHARD_TOTAL)
    boost = jnp.where(shard_of[None, :] == paired[:, None], 3.0, 1.0)
    values = values * rising[None, None, :, None] * group_scale[None, :, None, None] * boost[:, None, :, None]
    return jnp.clip(values, -100.0, 100.0).astype(jnp.bfloat16)


def levels(key, extent, shards, least, largest):
    gain = 1.0
    for axis_at, blocks in shards:
        steps = jax.random.uniform(jax.random.fold_in(jax.random.fold_in(key, 6), axis_at), (blocks,), jnp.float32, least / len(shards), largest / len(shards))
        gain = gain * jnp.repeat(jnp.exp(steps), extent[axis_at] // blocks).reshape((-1,) + (1,) * (len(extent) - 1 - axis_at))
    return gain


def noise(own_key, dims, scale, bound, cuts=(), dtype=jnp.bfloat16):
    result = scale * jax.random.normal(own_key, dims, jnp.float32)
    if cuts:
        result = result * levels(own_key, dims, cuts, -0.22, 0.18)
    return jnp.clip(result, -bound, bound).astype(dtype)


def setup_inputs(seed: int = 0) -> dict:
    seeds = jax.random.split(jax.random.key(seed), 9)
    master_old = noise(seeds[0], (SHARD_TOTAL, GROUPS, BLK_DEV, BLOCK), 0.25, 1.5, ((0, 8), (1, 4)), jnp.float32)
    m_codes = jnp.clip(jax.random.uniform(seeds[1], (SHARD_TOTAL, GROUPS, BLK_DEV, BLOCK), jnp.float32, -1.0, 1.0) * levels(seeds[1], (SHARD_TOTAL, GROUPS, BLK_DEV, BLOCK), ((0, 8), (1, 4)), -0.4, 0.0), -1.0, 1.0).astype(jnp.bfloat16)
    m_scale = jnp.clip(jnp.exp(math.log(0.5) - 2.3025851 * jax.random.uniform(seeds[2], (SHARD_TOTAL, GROUPS, BLK_DEV), jnp.float32) ** levels(seeds[2], (SHARD_TOTAL, GROUPS, BLK_DEV), ((0, 8), (1, 4)), -0.2, 0.2)), 0.05, 0.5)
    v_codes = jnp.clip(0.049804688 + 0.9501953 * jax.random.uniform(seeds[3], (SHARD_TOTAL, GROUPS, BLK_DEV, BLOCK), jnp.float32) ** levels(seeds[3], (SHARD_TOTAL, GROUPS, BLK_DEV, BLOCK), ((0, 8), (1, 4)), -0.2, 0.2), 0.049804688, 1.0).astype(jnp.bfloat16)
    v_scale = jnp.clip(jnp.exp(math.log(1.0) - 2.3025851 * jax.random.uniform(seeds[4], (SHARD_TOTAL, GROUPS, BLK_DEV), jnp.float32) ** levels(seeds[4], (SHARD_TOTAL, GROUPS, BLK_DEV), ((0, 8), (1, 4)), -0.2, 0.2)), 0.1, 1.0)
    grad_parts = draw_grad_parts(jax.random.fold_in(seeds[8], 71), 0)
    send_order = jax.vmap(lambda own: jax.random.permutation(own, BLK_DEV))(jax.random.split(seeds[6], SHARD_TOTAL * GROUPS)).reshape((SHARD_TOTAL, GROUPS, BLK_DEV)).astype(jnp.int32)
    recv_place = jax.vmap(lambda own: jax.random.permutation(own, BLK_DEV))(jax.random.split(seeds[7], SHARD_TOTAL * GROUPS)).reshape((SHARD_TOTAL, GROUPS, BLK_DEV)).astype(jnp.int32)
    return dict(master_old=master_old, m_codes=m_codes, m_scale=m_scale, v_codes=v_codes, v_scale=v_scale, grad_parts=grad_parts, send_order=send_order, recv_place=recv_place)


BETA_ONE = 0.9
BETA_TWO = 0.999
ADAM_EPS = 1e-08
LEARN_RATE = 0.05
DECAY_RATE = 0.1
CLIP_RMS = 1.0
QUANT_EPS = 1e-06
NORM_EPS = 1e-06

def dequant(codes, scales):
    return codes.astype(jnp.float32) * scales[..., None]

def requant(moment):
    magnitude = lax.optimization_barrier(jnp.max(jnp.abs(moment), axis=-1)) + QUANT_EPS
    return ((moment / magnitude[..., None]).astype(jnp.bfloat16), magnitude)

def widen_index(order, values):
    extra = values.ndim - 3
    shaped = order.reshape(order.shape + (1,) * extra)
    return jnp.broadcast_to(shaped, order.shape + values.shape[3:])

def relay_blocks(values, send_order, recv_place):
    shard_count, group_count, block_count = send_order.shape
    slot_size = block_count // group_count
    picked = jnp.take_along_axis(values, widen_index(send_order, values), axis=2)
    picked = picked.reshape((shard_count, group_count, group_count, slot_size) + values.shape[3:])
    arrived = jnp.swapaxes(picked, 1, 2).reshape(values.shape)
    inverse = jnp.argsort(recv_place, axis=-1).astype(jnp.int32)
    placed = jnp.take_along_axis(arrived, widen_index(inverse, arrived), axis=2)
    placed = jnp.swapaxes(placed, 0, 1)
    return placed.reshape((group_count, shard_count * block_count) + values.shape[3:])

def reference(master_old, m_codes, m_scale, v_codes, v_scale, grad_parts, send_order, recv_place):
    master = relay_blocks(master_old, send_order, recv_place)
    moment_one = relay_blocks(dequant(m_codes, m_scale), send_order, recv_place)
    moment_two = relay_blocks(dequant(v_codes, v_scale), send_order, recv_place)

    def accumulate(total, piece):
        return (total + piece.astype(jnp.float32), None)
    gradient, unused_out = lax.scan(accumulate, jnp.zeros(grad_parts.shape[1:], jnp.float32), grad_parts)
    total_squares = jnp.sum(gradient * gradient)
    root_mean = jnp.sqrt(total_squares / gradient.size + NORM_EPS)
    clip_factor = jnp.minimum(1.0, CLIP_RMS / root_mean)
    clipped = clip_factor * gradient
    m_next = BETA_ONE * moment_one + (1.0 - BETA_ONE) * clipped
    v_next = BETA_TWO * moment_two + (1.0 - BETA_TWO) * clipped * clipped
    bias_one = 1.0 - BETA_ONE ** STEP
    bias_two = 1.0 - BETA_TWO ** STEP
    update = m_next / bias_one / (jnp.sqrt(v_next / bias_two) + ADAM_EPS)
    master_new = master - LEARN_RATE * (update + DECAY_RATE * master)
    m_codes_new, m_scale_new = requant(m_next)
    v_codes_new, v_scale_new = requant(v_next)
    return (master_new, m_codes_new, m_scale_new, v_codes_new, v_scale_new)
```

```python
import functools

import jax
import jax.numpy as jnp
from jax import lax
from jax.experimental import pallas as pl
from jax.experimental.pallas import tpu as pltpu
from jax.sharding import PartitionSpec as P

STEP = 200

BETA_ONE = 0.9
BETA_TWO = 0.999
ADAM_EPS = 1e-08
LEARN_RATE = 0.05
DECAY_RATE = 0.1
CLIP_RMS = 1.0
QUANT_EPS = 1e-06
NORM_EPS = 1e-06

MESH = pl.DeviceIdType.MESH
UNROLL = 40
SUBLANES = 8
EIGHT = 8


def each(first, last, step):
    if last - first <= UNROLL:
        for k in range(first, last):
            step(k)
    else:
        lax.fori_loop(first, last, lambda k, c: (step(k), c)[1], 0)


def kernel(
    shards, groups,
    master_in, mc_in, ms_in, vc_in, vs_in, grads_in, order_in, place_in,
    state_out, lanes_out,
    master_v, mc_v, vc_v, m_wide, v_wide,
    ms_s, vs_s, order_s, place_s,
    relay_out, relay_in, whole_in, half_in, slim_in, far_out, far_in,
    square_out, mixed_out, square_in, second_in, square_all,
    in_sems, grad_sems, half_sems, relay_sems, far_sems, square_sems, second_sems,
):
    d = lax.axis_index("dp")
    e = lax.axis_index("expert")
    blocks, block = master_v.shape
    q = blocks // groups
    eights = shards // EIGHT
    per = groups - 1
    summers = per * eights
    odd = lax.rem(e, 2)
    pair = e // 2
    eight = d // EIGHT
    step = lax.rem(d, EIGHT)
    base = EIGHT * eight
    both = jnp.logical_and
    no = jnp.logical_not
    first = e < 2
    later = e >= 2
    chief = both(e == 1, step == 0)
    second = both(e == 1, step == 2)
    aide = both(both(odd == 1, later), jnp.logical_or(step == 0, step == 2))
    slot = eight * per + jnp.where(chief, 0, 2 * pair - 1 + step // 2)

    barrier = pltpu.get_barrier_semaphore()

    def greet(shard, group):
        pl.semaphore_signal(barrier, inc=1, device_id=(shard, group), device_id_type=MESH)

    @pl.when(chief)
    def _():
        each(0, shards, lambda k: [greet(lax.rem(d + k, shards), g) for g in range(2, groups)])

    @pl.when(jnp.logical_or(second, aide))
    def _():
        greet(d, e - 1)
        each(1, shards, lambda k: [greet(lax.rem(d + k, shards), e - g) for g in range(2)])

    @pl.when(e == 0)
    def _():
        greet(d, 3)

    @pl.when(both(e != 0, e != 2))
    def _():
        greet(d, 2)

    greeters = (
        jnp.where(first, eights, 3 * eights)
        - jnp.logical_or(second, aide).astype(jnp.int32)
        + jnp.where(e == 2, groups - 2, jnp.where(e == 3, 1, 0)))

    @pl.when(greeters > 0)
    def _():
        pl.semaphore_wait(barrier, greeters)

    source = odd * shards + d

    def send(src, dst, shard, group):
        @pl.when(jnp.logical_or(d != shard, e != group))
        def _():
            pltpu.make_async_remote_copy(
                src_ref=src, dst_ref=dst, send_sem=grad_sems.at[0], recv_sem=grad_sems.at[1],
                device_id=(shard, group), device_id_type=MESH).start()

    def send_first(i):
        send(grads_in.at[i], whole_in.at[source], EIGHT * i + 2, 1)

    def send_slim(i):
        send(grads_in.at[i, pl.ds(6, 2)], slim_in.at[source], EIGHT * i + 2, 2 * pair + 1)
        send(grads_in.at[i, pl.ds(4, 2)], slim_in.at[source], EIGHT * i, 2 * pair + 1)

    def send_half(i):
        pltpu.make_async_remote_copy(
            src_ref=grads_in.at[i, pl.ds(0, 4)], dst_ref=half_in.at[(e - 2) * shards + d],
            send_sem=half_sems.at[0], recv_sem=half_sems.at[1],
            device_id=(EIGHT * i, 1), device_id_type=MESH).start()

    @pl.when(first)
    def _():
        each(0, eights, send_first)

    @pl.when(later)
    def _():
        each(0, eights, send_slim)
        each(0, eights, send_half)

    def own_first():
        return pltpu.make_async_copy(grads_in.at[eight], whole_in.at[shards + d], in_sems.at[7])

    def own_slim():
        return pltpu.make_async_copy(
            grads_in.at[eight, pl.ds(4 + step, 2)], slim_in.at[shards + d], in_sems.at[7])

    @pl.when(second)
    def _():
        own_first().start()

    @pl.when(aide)
    def _():
        own_slim().start()

    loads = [
        pltpu.make_async_copy(src, dst, in_sems.at[i])
        for i, (src, dst) in enumerate((
            (order_in, order_s), (ms_in, ms_s), (vs_in, vs_s),
            (mc_in, mc_v), (vc_in, vc_v), (master_in, master_v), (place_in, place_s),
        ))
    ]
    for load in loads:
        load.start()
    for load in loads:
        load.wait()
    m_wide[...] = mc_v[...].astype(jnp.float32)
    v_wide[...] = vc_v[...].astype(jnp.float32)

    def relay_copy(k, sem):
        return pltpu.make_async_remote_copy(
            src_ref=relay_out.at[k], dst_ref=relay_in.at[k - 1],
            send_sem=relay_sems.at[0], recv_sem=relay_sems.at[sem],
            device_id=(d, lax.rem(e + k, groups)), device_id_type=MESH)

    for k in range(groups):
        to = lax.rem(e + k, groups)
        for c in range(q):
            row = order_s[0, to * q + c]
            relay_out[k, 0, c : c + 1, :] = master_v[pl.ds(row, 1), :]
            relay_out[k, 1, c : c + 1, :] = m_wide[pl.ds(row, 1), :] * ms_s[0, row]
            relay_out[k, 2, c : c + 1, :] = v_wide[pl.ds(row, 1), :] * vs_s[0, row]

    @pl.when(e == 2)
    def _():
        relay_copy(1, 3).start()

    @pl.when(e == 3)
    def _():
        relay_copy(1, 3).wait_recv()
        for k in range(1, groups):
            relay_copy(k, 2).start()

    @pl.when(e != 3)
    def _():
        relay_copy(1, 2).wait_recv()
        for k in range(2, groups):
            relay_copy(k, 1).start()

        @pl.when(e != 2)
        def _():
            relay_copy(1, 1).start()

    def some(ref, count, sems):
        part = ref.at[pl.ds(0, count)]
        return pltpu.make_async_remote_copy(
            src_ref=part, dst_ref=part, send_sem=sems.at[0], recv_sem=sems.at[1],
            device_id=(d, lax.rem(e + 1, groups)), device_id_type=MESH)

    def total(arrived, begin):
        if shards <= UNROLL:
            gradient = arrived[begin].astype(jnp.float32)
            for k in range(1, shards):
                gradient = gradient + arrived[begin + k].astype(jnp.float32)
            return gradient
        return lax.fori_loop(
            0, shards, lambda k, g: g + arrived[begin + k].astype(jnp.float32),
            jnp.zeros(arrived.shape[1:], jnp.float32))

    def finish(parts, out, mine):
        squares = jnp.zeros((SUBLANES, block), jnp.float32)
        for gradient, at in parts:
            squares = squares + jnp.sum((gradient * gradient).reshape(-1, SUBLANES, block), axis=0)
            far_out[pl.ds(at, gradient.shape[0])] = gradient
        squares = jnp.sum(squares, axis=0, keepdims=True)
        out[...] = squares
        mine[...] = squares

    def send_square(shard, group, out=square_out, to=square_in.at[slot], sems=square_sems):
        pltpu.make_async_remote_copy(
            src_ref=out, dst_ref=to, send_sem=sems.at[0], recv_sem=sems.at[1],
            device_id=(shard, group), device_id_type=MESH).start()

    def send_second(shard, group):
        send_square(shard, group, square_out, second_in.at[eight], second_sems)

    def send_mixed(shard, group):
        send_square(shard, group, mixed_out)

    def send_far(at, shard, group):
        pltpu.make_async_remote_copy(
            src_ref=far_out.at[at], dst_ref=far_in.at[0],
            send_sem=far_sems.at[0], recv_sem=far_sems.at[1],
            device_id=(shard, group), device_id_type=MESH).start()

    def row(k):
        return lax.rem(base + k, shards)

    @pl.when(second)
    def _():
        own_first().wait()
        some(whole_in, 2 * shards - 1, grad_sems).wait_recv()
        finish([(total(whole_in, g * shards), g * EIGHT) for g in range(2)], square_out, second_in.at[eight])
        for k in range(EIGHT):
            for g in range(2):
                if k != 2 or g != 1:
                    send_second(base + k, g)
        for k in range(EIGHT):
            for g in range(2):
                if k != 2 or g != 1:
                    send_far(g * EIGHT + k, base + k, g)
        each(EIGHT, shards, lambda k: [send_second(row(k), g) for g in range(2)])

    @pl.when(chief)
    def _():
        some(half_in, (groups - 2) * shards, half_sems).wait_recv()
        finish([(total(half_in, g * shards), g * 4) for g in range(groups - 2)], square_out, square_in.at[slot])
        send_square(d, 0)
        some(second_in, eights, second_sems).wait_recv()
        mixed_out[...] = square_out[...] + second_in[eight]
        for k in range(4):
            for g in range(2, groups):
                send_far((g - 2) * 4 + k, base + k, g)
                send_mixed(base + k, g)
        for k in range(1, EIGHT):
            for g in range(2):
                send_square(base + k, g)
        for k in range(4, EIGHT):
            for g in range(2, groups):
                send_mixed(base + k, g)

        def rest(k):
            for g in range(2):
                send_square(row(k), g)
            for g in range(2, groups):
                send_mixed(row(k), g)

        each(EIGHT, shards, rest)

    @pl.when(aide)
    def _():
        own_slim().wait()
        some(slim_in, 2 * shards - 1, grad_sems).wait_recv()
        finish([(total(slim_in, g * shards), g * 2) for g in range(2)], square_out, square_in.at[slot])

        def send_row(k):
            for g in range(groups):
                @pl.when(jnp.logical_or(step != k, e != g))
                def _():
                    send_square(base + k, g)

        send_row(0)
        for j in range(2):
            for g in range(2):
                send_far(g * 2 + j, base + 4 + step + j, e - 1 + g)
        send_row(2)
        for k in (1, 3, 4, 5, 6, 7):
            for g in range(groups):
                send_square(base + k, g)
        each(EIGHT, shards, lambda k: [send_square(row(k), g) for g in range(groups)])

    relay_whole = some(relay_in, groups - 1, relay_sems)

    some(relay_in, groups - 2, relay_sems).wait_recv()
    rows = lax.broadcasted_iota(jnp.int32, (blocks, block), 0)
    placed = [jnp.zeros((blocks, block), jnp.float32) for _ in range(3)]
    for k in range(groups):
        frm = lax.rem(e - k + groups, groups)
        for c in range(q):
            here = rows == place_s[0, frm * q + c]
            for i in range(3):
                row = relay_out[0, i, c : c + 1, :] if k == 0 else relay_in[k - 1, i, c : c + 1, :]
                placed[i] = jnp.where(here, jnp.broadcast_to(row, (blocks, block)), placed[i])
    for i in range(3):
        state_out[i + 1] = placed[i]

    @pl.when(second)
    def _():
        state_out[0] = far_out[EIGHT + 2]

    @pl.when(no(second))
    def _():
        some(far_in, 1, far_sems).wait_recv()
        state_out[0] = far_in[0]

    sums = jnp.logical_or(chief, aide)

    @pl.when(sums)
    def _():
        some(square_in, summers - 1, square_sems).wait_recv()

    @pl.when(no(sums))
    def _():
        some(square_in, summers, square_sems).wait_recv()

    if eights > 1:
        @pl.when(second)
        def _():
            some(second_in, eights - 1, second_sems).wait_recv()

    @pl.when(both(first, no(jnp.logical_or(chief, second))))
    def _():
        some(second_in, eights, second_sems).wait_recv()

    squares = jnp.sum(square_in[...], axis=0)

    @pl.when(first)
    def _():
        lanes_out[...] = squares + jnp.sum(second_in[...], axis=0)

    @pl.when(later)
    def _():
        lanes_out[...] = squares

    relay_whole.wait_send()

    if eights > 1:
        @pl.when(second)
        def _():
            some(whole_in, eights - 1, grad_sems).wait_send()

    @pl.when(second)
    def _():
        some(square_all, 2 * shards - 1, second_sems).wait_send()
        some(far_out, 2 * EIGHT - 1, far_sems).wait_send()

    @pl.when(both(first, no(second)))
    def _():
        some(whole_in, eights, grad_sems).wait_send()

    @pl.when(later)
    def _():
        some(half_in, eights, half_sems).wait_send()

    @pl.when(chief)
    def _():
        some(square_all, shards * groups - 1, square_sems).wait_send()
        some(far_out, 4 * (groups - 2), far_sems).wait_send()

    @pl.when(aide)
    def _():
        some(slim_in, 2 * eights - 1, grad_sems).wait_send()
        some(square_all, shards * groups - 1, square_sems).wait_send()
        some(far_out, 4, far_sems).wait_send()

    @pl.when(both(later, no(aide)))
    def _():
        some(slim_in, 2 * eights, grad_sems).wait_send()


def update(count, state, lanes, master_out, mc_out, ms_out, vc_out, vs_out):
    gradient, master, moment_one, moment_two = (state[i] for i in range(4))
    blocks, block = gradient.shape

    total_squares = jnp.sum(lanes[...], axis=1, keepdims=True)
    root_mean = jnp.sqrt(total_squares / count + NORM_EPS)
    clip_factor = jnp.minimum(1.0, CLIP_RMS / root_mean)

    clipped = clip_factor * gradient
    m_next = BETA_ONE * moment_one + (1.0 - BETA_ONE) * clipped
    v_next = BETA_TWO * moment_two + (1.0 - BETA_TWO) * clipped * clipped
    bias_one = 1.0 - BETA_ONE**STEP
    bias_two = 1.0 - BETA_TWO**STEP
    m_mag = jnp.max(jnp.abs(m_next), axis=1, keepdims=True) + QUANT_EPS
    v_mag = jnp.max(jnp.abs(v_next), axis=1, keepdims=True) + QUANT_EPS
    step = m_next / bias_one / (jnp.sqrt(v_next / bias_two) + ADAM_EPS)
    master_out[...] = master - LEARN_RATE * (step + DECAY_RATE * master)
    mc_out[...] = (m_next / m_mag).astype(jnp.bfloat16)
    vc_out[...] = (v_next / v_mag).astype(jnp.bfloat16)
    rows = lax.broadcasted_iota(jnp.int32, (blocks, block), 0)
    diagonal = rows == lax.broadcasted_iota(jnp.int32, (blocks, block), 1)
    ms_out[...] = jnp.sum(jnp.where(diagonal, m_mag, 0.0), axis=0, keepdims=True)[:, :blocks]
    vs_out[...] = jnp.sum(jnp.where(diagonal, v_mag, 0.0), axis=0, keepdims=True)[:, :blocks]


def body(shards, groups, master_old, m_codes, m_scale, v_codes, v_scale, grad_parts, send_order, recv_place):
    blocks, block = master_old.shape[2:]
    eights = shards // EIGHT
    summers = (groups - 1) * eights
    owners = max(2 * EIGHT, 4 * (groups - 2))
    f32, bf16 = jnp.float32, jnp.bfloat16
    wide = (blocks, block)
    anywhere = pl.BlockSpec(memory_space=pl.ANY)
    vmem = pl.BlockSpec(memory_space=pltpu.VMEM)
    state, lanes = pl.pallas_call(
        functools.partial(kernel, shards, groups),
        out_shape=(pltpu.VMEM((4, blocks, block), f32), pltpu.VMEM((1, block), f32)),
        in_specs=[anywhere] * 8,
        out_specs=(vmem, vmem),
        scratch_shapes=[
            pltpu.VMEM(wide, f32),
            pltpu.VMEM(wide, bf16),
            pltpu.VMEM(wide, bf16),
            pltpu.VMEM(wide, f32),
            pltpu.VMEM(wide, f32),
            pltpu.SMEM((1, blocks), f32),
            pltpu.SMEM((1, blocks), f32),
            pltpu.SMEM((1, blocks), jnp.int32),
            pltpu.SMEM((1, blocks), jnp.int32),
            pltpu.VMEM((groups, 3, blocks // groups, block), f32),
            pltpu.VMEM((groups - 1, 3, blocks // groups, block), f32),
            pltpu.VMEM((2 * shards, EIGHT, blocks, block), bf16),
            pltpu.VMEM(((groups - 2) * shards, 4, blocks, block), bf16),
            pltpu.VMEM((2 * shards, 2, blocks, block), bf16),
            pltpu.VMEM((owners, blocks, block), f32),
            pltpu.VMEM((1, blocks, block), f32),
            pltpu.VMEM((1, block), f32),
            pltpu.VMEM((1, block), f32),
            pltpu.VMEM((summers, 1, block), f32),
            pltpu.VMEM((eights, 1, block), f32),
            pltpu.VMEM((shards * groups - 1, 1, block), f32),
            pltpu.SemaphoreType.DMA((8,)),
            pltpu.SemaphoreType.DMA((2,)),
            pltpu.SemaphoreType.DMA((2,)),
            pltpu.SemaphoreType.DMA((4,)),
            pltpu.SemaphoreType.DMA((2,)),
            pltpu.SemaphoreType.DMA((2,)),
            pltpu.SemaphoreType.DMA((2,)),
        ],
        compiler_params=pltpu.CompilerParams(collective_id=0, has_side_effects=True),
    )(
        master_old.reshape(wide), m_codes.reshape(wide), m_scale.reshape(1, blocks),
        v_codes.reshape(wide), v_scale.reshape(1, blocks),
        grad_parts.reshape(eights, EIGHT, blocks, block),
        send_order.reshape(1, blocks), recv_place.reshape(1, blocks),
    )
    master_new, mc, ms, vc, vs = pl.pallas_call(
        functools.partial(update, shards * groups * blocks * block),
        out_shape=(
            jax.ShapeDtypeStruct(wide, f32),
            jax.ShapeDtypeStruct(wide, bf16),
            jax.ShapeDtypeStruct((1, blocks), f32),
            jax.ShapeDtypeStruct(wide, bf16),
            jax.ShapeDtypeStruct((1, blocks), f32),
        ),
        in_specs=[vmem, vmem],
        out_specs=(vmem,) * 5,
    )(
        pltpu.with_memory_space_constraint(state, pltpu.VMEM),
        pltpu.with_memory_space_constraint(lanes, pltpu.VMEM))
    return master_new[None], mc[None], ms, vc[None], vs


def solution(mesh):
    rows = P("dp", "expert", None, None)
    flat = P("dp", "expert", None)
    return jax.shard_map(
        functools.partial(body, mesh.shape["dp"], mesh.shape["expert"]),
        mesh=mesh,
        in_specs=(rows, rows, flat, rows, flat, rows, flat, flat),
        out_specs=(
            P("expert", "dp", None),
            P("expert", "dp", None),
            P("expert", "dp"),
            P("expert", "dp", None),
            P("expert", "dp"),
        ),
        check_vma=False,
    )
```

```python
import functools

import jax
import jax.numpy as jnp
from jax import lax
from jax.experimental import pallas as pl
from jax.experimental.pallas import tpu as pltpu
from jax.sharding import PartitionSpec as P

STEP = 200

BETA_ONE = 0.9
BETA_TWO = 0.999
ADAM_EPS = 1e-08
LEARN_RATE = 0.05
DECAY_RATE = 0.1
CLIP_RMS = 1.0
QUANT_EPS = 1e-06
NORM_EPS = 1e-06

MESH = pl.DeviceIdType.MESH
UNROLL = 40
SUBLANES = 8
EIGHT = 8


def each(first, last, step):
    if last - first <= UNROLL:
        for k in range(first, last):
            step(k)
    else:
        lax.fori_loop(first, last, lambda k, c: (step(k), c)[1], 0)


def kernel(
    shards, groups,
    master_in, mc_in, ms_in, vc_in, vs_in, grads_in, order_in, place_in,
    state_out, lanes_out,
    master_v, mc_v, vc_v, m_wide, v_wide,
    ms_s, vs_s, order_s, place_s,
    relay_out, relay_in, whole_in, half_in, slim_in, far_out, far_in,
    square_out, mixed_out, square_in, second_in, square_all,
    in_sems, grad_sems, half_sems, relay_sems, far_sems, square_sems, second_sems,
):
    d = lax.axis_index("dp")
    e = lax.axis_index("expert")
    blocks, block = master_v.shape
    q = blocks // groups
    eights = shards // EIGHT
    per = groups - 1
    summers = per * eights
    odd = lax.rem(e, 2)
    pair = e // 2
    eight = d // EIGHT
    step = lax.rem(d, EIGHT)
    base = EIGHT * eight
    both = jnp.logical_and
    no = jnp.logical_not
    first = e < 2
    later = e >= 2
    chief = both(e == 1, step == 0)
    second = both(e == 1, step == 2)
    aide = both(both(odd == 1, later), jnp.logical_or(step == 0, step == 2))
    last = d == shards - 1
    spared = both(last, e == 0)
    bridge = both(last, e == 1)
    leader = jnp.where(last, 1, 3)
    slot = eight * per + jnp.where(chief, 0, 2 * pair - 1 + step // 2)

    barrier = pltpu.get_barrier_semaphore()

    def greet(shard, group):
        pl.semaphore_signal(barrier, inc=1, device_id=(shard, group), device_id_type=MESH)

    @pl.when(chief)
    def _():
        each(0, shards, lambda k: [greet(lax.rem(d + k, shards), g) for g in range(2, groups)])

    @pl.when(jnp.logical_or(second, aide))
    def _():
        greet(d, e - 1)
        each(1, shards, lambda k: [greet(lax.rem(d + k, shards), e - g) for g in range(2)])

    @pl.when(e == 0)
    def _():
        greet(d, leader)

    @pl.when(both(e != 0, e != 2))
    def _():
        greet(d, 2)

    greeters = (
        jnp.where(first, eights, 3 * eights)
        - jnp.logical_or(second, aide).astype(jnp.int32)
        + jnp.where(e == 2, groups - 2, jnp.where(e == leader, 1, 0)))

    @pl.when(greeters > 0)
    def _():
        pl.semaphore_wait(barrier, greeters)

    source = odd * shards + d

    def send(src, dst, shard, group):
        @pl.when(jnp.logical_or(d != shard, e != group))
        def _():
            pltpu.make_async_remote_copy(
                src_ref=src, dst_ref=dst, send_sem=grad_sems.at[0], recv_sem=grad_sems.at[1],
                device_id=(shard, group), device_id_type=MESH).start()

    def send_first(i):
        send(grads_in.at[i], whole_in.at[source], EIGHT * i + 2, 1)

    def send_slim(i):
        send(grads_in.at[i, pl.ds(6, 2)], slim_in.at[source], EIGHT * i + 2, 2 * pair + 1)
        send(grads_in.at[i, pl.ds(4, 2)], slim_in.at[source], EIGHT * i, 2 * pair + 1)

    def send_half(i):
        pltpu.make_async_remote_copy(
            src_ref=grads_in.at[i, pl.ds(0, 4)], dst_ref=half_in.at[(e - 2) * shards + d],
            send_sem=half_sems.at[0], recv_sem=half_sems.at[1],
            device_id=(EIGHT * i, 1), device_id_type=MESH).start()

    @pl.when(first)
    def _():
        each(0, eights, send_first)

    @pl.when(later)
    def _():
        each(0, eights, send_slim)
        each(0, eights, send_half)

    def own_first():
        return pltpu.make_async_copy(grads_in.at[eight], whole_in.at[shards + d], in_sems.at[7])

    def own_slim():
        return pltpu.make_async_copy(
            grads_in.at[eight, pl.ds(4 + step, 2)], slim_in.at[shards + d], in_sems.at[7])

    @pl.when(second)
    def _():
        own_first().start()

    @pl.when(aide)
    def _():
        own_slim().start()

    loads = [
        pltpu.make_async_copy(src, dst, in_sems.at[i])
        for i, (src, dst) in enumerate((
            (order_in, order_s), (ms_in, ms_s), (vs_in, vs_s),
            (mc_in, mc_v), (vc_in, vc_v), (master_in, master_v), (place_in, place_s),
        ))
    ]
    for load in loads:
        load.start()
    for load in loads:
        load.wait()
    m_wide[...] = mc_v[...].astype(jnp.float32)
    v_wide[...] = vc_v[...].astype(jnp.float32)

    def relay_copy(k, sem):
        return pltpu.make_async_remote_copy(
            src_ref=relay_out.at[k], dst_ref=relay_in.at[k - 1],
            send_sem=relay_sems.at[0], recv_sem=relay_sems.at[sem],
            device_id=(d, lax.rem(e + k, groups)), device_id_type=MESH)

    for k in range(groups):
        to = lax.rem(e + k, groups)
        for c in range(q):
            row = order_s[0, to * q + c]
            relay_out[k, 0, c : c + 1, :] = master_v[pl.ds(row, 1), :]
            relay_out[k, 1, c : c + 1, :] = m_wide[pl.ds(row, 1), :] * ms_s[0, row]
            relay_out[k, 2, c : c + 1, :] = v_wide[pl.ds(row, 1), :] * vs_s[0, row]

    to_leader = lax.rem(leader - 2 + groups, groups)

    @pl.when(e == 2)
    def _():
        relay_copy(to_leader, 3).start()

    @pl.when(e == leader)
    def _():
        relay_copy(to_leader, 3).wait_recv()
        for k in range(1, groups):
            relay_copy(k, 2).start()

    @pl.when(e != leader)
    def _():
        relay_copy(1, 2).wait_recv()
        for k in range(1, groups):
            @pl.when(jnp.logical_or(e != 2, k != to_leader))
            def _():
                relay_copy(k, 1).start()

    def some(ref, count, sems):
        part = ref.at[pl.ds(0, count)]
        return pltpu.make_async_remote_copy(
            src_ref=part, dst_ref=part, send_sem=sems.at[0], recv_sem=sems.at[1],
            device_id=(d, lax.rem(e + 1, groups)), device_id_type=MESH)

    def total(arrived, begin):
        if shards <= UNROLL:
            gradient = arrived[begin].astype(jnp.float32)
            for k in range(1, shards):
                gradient = gradient + arrived[begin + k].astype(jnp.float32)
            return gradient
        return lax.fori_loop(
            0, shards, lambda k, g: g + arrived[begin + k].astype(jnp.float32),
            jnp.zeros(arrived.shape[1:], jnp.float32))

    def finish(parts, out, mine):
        squares = jnp.zeros((SUBLANES, block), jnp.float32)
        for gradient, at in parts:
            squares = squares + jnp.sum((gradient * gradient).reshape(-1, SUBLANES, block), axis=0)
            far_out[pl.ds(at, gradient.shape[0])] = gradient
        squares = jnp.sum(squares, axis=0, keepdims=True)
        out[...] = squares
        mine[...] = squares

    def send_square(shard, group, out=square_out, to=square_in.at[slot], sems=square_sems):
        def start():
            pltpu.make_async_remote_copy(
                src_ref=out, dst_ref=to, send_sem=sems.at[0], recv_sem=sems.at[1],
                device_id=(shard, group), device_id_type=MESH).start()

        if isinstance(group, int) and group == 0:
            pl.when(shard != shards - 1)(start)
        else:
            start()

    def send_second(shard, group):
        send_square(shard, group, square_out, second_in.at[eight], second_sems)

    def send_mixed(shard, group):
        send_square(shard, group, mixed_out)

    def send_far(at, shard, group):
        pltpu.make_async_remote_copy(
            src_ref=far_out.at[at], dst_ref=far_in.at[0],
            send_sem=far_sems.at[0], recv_sem=far_sems.at[1],
            device_id=(shard, group), device_id_type=MESH).start()

    def row(k):
        return lax.rem(base + k, shards)

    @pl.when(second)
    def _():
        own_first().wait()
        some(whole_in, 2 * shards - 1, grad_sems).wait_recv()
        finish([(total(whole_in, g * shards), g * EIGHT) for g in range(2)], square_out, second_in.at[eight])
        for k in range(EIGHT):
            for g in range(2):
                if k != 2 or g != 1:
                    send_second(base + k, g)
        for k in range(EIGHT):
            for g in range(2):
                if k != 2 or g != 1:
                    send_far(g * EIGHT + k, base + k, g)
        each(EIGHT, shards, lambda k: [send_second(row(k), g) for g in range(2)])

    @pl.when(chief)
    def _():
        some(half_in, (groups - 2) * shards, half_sems).wait_recv()
        finish([(total(half_in, g * shards), g * 4) for g in range(groups - 2)], square_out, square_in.at[slot])
        send_square(d, 0)
        some(second_in, eights, second_sems).wait_recv()
        mixed_out[...] = square_out[...] + second_in[eight]
        for k in range(4):
            for g in range(2, groups):
                send_far((g - 2) * 4 + k, base + k, g)
                send_mixed(base + k, g)
        for k in range(1, EIGHT):
            for g in range(2):
                send_square(base + k, g)
        for k in range(4, EIGHT):
            for g in range(2, groups):
                send_mixed(base + k, g)

        def rest(k):
            for g in range(2):
                send_square(row(k), g)
            for g in range(2, groups):
                send_mixed(row(k), g)

        each(EIGHT, shards, rest)

    @pl.when(aide)
    def _():
        own_slim().wait()
        some(slim_in, 2 * shards - 1, grad_sems).wait_recv()
        finish([(total(slim_in, g * shards), g * 2) for g in range(2)], square_out, square_in.at[slot])

        def send_row(k):
            for g in range(groups):
                @pl.when(jnp.logical_or(step != k, e != g))
                def _():
                    send_square(base + k, g)

        send_row(0)
        for j in range(2):
            for g in range(2):
                send_far(g * 2 + j, base + 4 + step + j, e - 1 + g)
        send_row(2)
        for k in (1, 3, 4, 5, 6, 7):
            for g in range(groups):
                send_square(base + k, g)
        each(EIGHT, shards, lambda k: [send_square(row(k), g) for g in range(groups)])

    relay_whole = some(relay_in, groups - 1, relay_sems)

    some(relay_in, groups - 2, relay_sems).wait_recv()
    rows = lax.broadcasted_iota(jnp.int32, (blocks, block), 0)
    placed = [jnp.zeros((blocks, block), jnp.float32) for _ in range(3)]
    for k in range(groups):
        frm = lax.rem(e - k + groups, groups)
        for c in range(q):
            here = rows == place_s[0, frm * q + c]
            for i in range(3):
                row = relay_out[0, i, c : c + 1, :] if k == 0 else relay_in[k - 1, i, c : c + 1, :]
                placed[i] = jnp.where(here, jnp.broadcast_to(row, (blocks, block)), placed[i])
    for i in range(3):
        state_out[i + 1] = placed[i]

    @pl.when(second)
    def _():
        state_out[0] = far_out[EIGHT + 2]

    @pl.when(no(second))
    def _():
        some(far_in, 1, far_sems).wait_recv()
        state_out[0] = far_in[0]

    sums = jnp.logical_or(chief, aide)

    @pl.when(sums)
    def _():
        some(square_in, summers - 1, square_sems).wait_recv()

    @pl.when(no(jnp.logical_or(sums, spared)))
    def _():
        some(square_in, summers, square_sems).wait_recv()

    if eights > 1:
        @pl.when(second)
        def _():
            some(second_in, eights - 1, second_sems).wait_recv()

    @pl.when(both(both(first, no(spared)), no(jnp.logical_or(chief, second))))
    def _():
        some(second_in, eights, second_sems).wait_recv()

    @pl.when(later)
    def _():
        lanes_out[...] = jnp.sum(square_in[...], axis=0)

    @pl.when(both(first, no(spared)))
    def _():
        lanes_out[...] = jnp.sum(square_in[...], axis=0) + jnp.sum(second_in[...], axis=0)

    def bridge_copy():
        return pltpu.make_async_remote_copy(
            src_ref=mixed_out, dst_ref=second_in.at[0], send_sem=second_sems.at[0], recv_sem=second_sems.at[1],
            device_id=(d, 0), device_id_type=MESH)

    @pl.when(bridge)
    def _():
        mixed_out[...] = lanes_out[...]
        bridge_copy().start()

    @pl.when(spared)
    def _():
        bridge_copy().wait_recv()
        lanes_out[...] = second_in[0]

    relay_whole.wait_send()

    if eights > 1:
        @pl.when(second)
        def _():
            some(whole_in, eights - 1, grad_sems).wait_send()

    @pl.when(second)
    def _():
        some(square_all, 2 * shards - 2, second_sems).wait_send()
        some(far_out, 2 * EIGHT - 1, far_sems).wait_send()

    @pl.when(both(first, no(second)))
    def _():
        some(whole_in, eights, grad_sems).wait_send()

    @pl.when(later)
    def _():
        some(half_in, eights, half_sems).wait_send()

    @pl.when(chief)
    def _():
        some(square_all, shards * groups - 2, square_sems).wait_send()
        some(far_out, 4 * (groups - 2), far_sems).wait_send()

    @pl.when(aide)
    def _():
        some(slim_in, 2 * eights - 1, grad_sems).wait_send()
        some(square_all, shards * groups - 2, square_sems).wait_send()
        some(far_out, 4, far_sems).wait_send()

    @pl.when(both(later, no(aide)))
    def _():
        some(slim_in, 2 * eights, grad_sems).wait_send()

    @pl.when(bridge)
    def _():
        bridge_copy().wait_send()


def update(count, state, lanes, master_out, mc_out, ms_out, vc_out, vs_out):
    gradient, master, moment_one, moment_two = (state[i] for i in range(4))
    blocks, block = gradient.shape

    total_squares = jnp.sum(lanes[...], axis=1, keepdims=True)
    root_mean = jnp.sqrt(total_squares / count + NORM_EPS)
    clip_factor = jnp.minimum(1.0, CLIP_RMS / root_mean)

    clipped = clip_factor * gradient
    m_next = BETA_ONE * moment_one + (1.0 - BETA_ONE) * clipped
    v_next = BETA_TWO * moment_two + (1.0 - BETA_TWO) * clipped * clipped
    bias_one = 1.0 - BETA_ONE**STEP
    bias_two = 1.0 - BETA_TWO**STEP
    m_mag = jnp.max(jnp.abs(m_next), axis=1, keepdims=True) + QUANT_EPS
    v_mag = jnp.max(jnp.abs(v_next), axis=1, keepdims=True) + QUANT_EPS
    step = m_next / bias_one / (jnp.sqrt(v_next / bias_two) + ADAM_EPS)
    master_out[...] = master - LEARN_RATE * (step + DECAY_RATE * master)
    mc_out[...] = (m_next / m_mag).astype(jnp.bfloat16)
    vc_out[...] = (v_next / v_mag).astype(jnp.bfloat16)
    rows = lax.broadcasted_iota(jnp.int32, (blocks, block), 0)
    diagonal = rows == lax.broadcasted_iota(jnp.int32, (blocks, block), 1)
    ms_out[...] = jnp.sum(jnp.where(diagonal, m_mag, 0.0), axis=0, keepdims=True)[:, :blocks]
    vs_out[...] = jnp.sum(jnp.where(diagonal, v_mag, 0.0), axis=0, keepdims=True)[:, :blocks]


def body(shards, groups, master_old, m_codes, m_scale, v_codes, v_scale, grad_parts, send_order, recv_place):
    blocks, block = master_old.shape[2:]
    eights = shards // EIGHT
    summers = (groups - 1) * eights
    owners = max(2 * EIGHT, 4 * (groups - 2))
    f32, bf16 = jnp.float32, jnp.bfloat16
    wide = (blocks, block)
    anywhere = pl.BlockSpec(memory_space=pl.ANY)
    vmem = pl.BlockSpec(memory_space=pltpu.VMEM)
    state, lanes = pl.pallas_call(
        functools.partial(kernel, shards, groups),
        out_shape=(pltpu.VMEM((4, blocks, block), f32), pltpu.VMEM((1, block), f32)),
        in_specs=[anywhere] * 8,
        out_specs=(vmem, vmem),
        scratch_shapes=[
            pltpu.VMEM(wide, f32),
            pltpu.VMEM(wide, bf16),
            pltpu.VMEM(wide, bf16),
            pltpu.VMEM(wide, f32),
            pltpu.VMEM(wide, f32),
            pltpu.SMEM((1, blocks), f32),
            pltpu.SMEM((1, blocks), f32),
            pltpu.SMEM((1, blocks), jnp.int32),
            pltpu.SMEM((1, blocks), jnp.int32),
            pltpu.VMEM((groups, 3, blocks // groups, block), f32),
            pltpu.VMEM((groups - 1, 3, blocks // groups, block), f32),
            pltpu.VMEM((2 * shards, EIGHT, blocks, block), bf16),
            pltpu.VMEM(((groups - 2) * shards, 4, blocks, block), bf16),
            pltpu.VMEM((2 * shards, 2, blocks, block), bf16),
            pltpu.VMEM((owners, blocks, block), f32),
            pltpu.VMEM((1, blocks, block), f32),
            pltpu.VMEM((1, block), f32),
            pltpu.VMEM((1, block), f32),
            pltpu.VMEM((summers, 1, block), f32),
            pltpu.VMEM((eights, 1, block), f32),
            pltpu.VMEM((shards * groups - 2, 1, block), f32),
            pltpu.SemaphoreType.DMA((8,)),
            pltpu.SemaphoreType.DMA((2,)),
            pltpu.SemaphoreType.DMA((2,)),
            pltpu.SemaphoreType.DMA((4,)),
            pltpu.SemaphoreType.DMA((2,)),
            pltpu.SemaphoreType.DMA((2,)),
            pltpu.SemaphoreType.DMA((2,)),
        ],
        compiler_params=pltpu.CompilerParams(collective_id=0, has_side_effects=True),
    )(
        master_old.reshape(wide), m_codes.reshape(wide), m_scale.reshape(1, blocks),
        v_codes.reshape(wide), v_scale.reshape(1, blocks),
        grad_parts.reshape(eights, EIGHT, blocks, block),
        send_order.reshape(1, blocks), recv_place.reshape(1, blocks),
    )
    master_new, mc, ms, vc, vs = pl.pallas_call(
        functools.partial(update, shards * groups * blocks * block),
        out_shape=(
            jax.ShapeDtypeStruct(wide, f32),
            jax.ShapeDtypeStruct(wide, bf16),
            jax.ShapeDtypeStruct((1, blocks), f32),
            jax.ShapeDtypeStruct(wide, bf16),
            jax.ShapeDtypeStruct((1, blocks), f32),
        ),
        in_specs=[vmem, vmem],
        out_specs=(vmem,) * 5,
    )(
        pltpu.with_memory_space_constraint(state, pltpu.VMEM),
        pltpu.with_memory_space_constraint(lanes, pltpu.VMEM))
    return master_new[None], mc[None], ms, vc[None], vs


def solution(mesh):
    rows = P("dp", "expert", None, None)
    flat = P("dp", "expert", None)
    return jax.shard_map(
        functools.partial(body, mesh.shape["dp"], mesh.shape["expert"]),
        mesh=mesh,
        in_specs=(rows, rows, flat, rows, flat, rows, flat, flat),
        out_specs=(
            P("expert", "dp", None),
            P("expert", "dp", None),
            P("expert", "dp"),
            P("expert", "dp", None),
            P("expert", "dp"),
        ),
        check_vma=False,
    )
```

```python
import functools

import jax
import jax.numpy as jnp
from jax import lax
from jax.experimental import pallas as pl
from jax.experimental.pallas import tpu as pltpu
from jax.sharding import PartitionSpec as P

STEP = 200

BETA_ONE = 0.9
BETA_TWO = 0.999
ADAM_EPS = 1e-08
LEARN_RATE = 0.05
DECAY_RATE = 0.1
CLIP_RMS = 1.0
QUANT_EPS = 1e-06
NORM_EPS = 1e-06

MESH = pl.DeviceIdType.MESH
UNROLL = 40
SUBLANES = 8
EIGHT = 8
SPAN = EIGHT // 2


def each(first, last, step):
    if last - first <= UNROLL:
        for k in range(first, last):
            step(k)
    else:
        lax.fori_loop(first, last, lambda k, c: (step(k), c)[1], 0)


def kernel(
    shards, groups,
    master_in, mc_in, ms_in, vc_in, vs_in, grads_in, order_in, place_in,
    state_out, lanes_out,
    master_v, mc_v, vc_v, m_wide, v_wide,
    ms_s, vs_s, order_s, place_s,
    relay_out, relay_in, whole_in, wide_in, slim_in, far_out, far_in,
    wide_sum, square_out, mixed_out, square_in, second_in, square_all,
    in_sems, grad_sems, slim_sems, wide_sems, relay_sems, far_sems, square_sems, second_sems,
):
    d = lax.axis_index("dp")
    e = lax.axis_index("expert")
    blocks, block = master_v.shape
    q = blocks // groups
    eights = shards // EIGHT
    odd = lax.rem(e, 2)
    pair = e // 2
    eight = d // EIGHT
    step = lax.rem(d, EIGHT)
    base = EIGHT * eight
    both = jnp.logical_and
    no = jnp.logical_not
    first = e < 2
    later = e >= 2
    chief = both(e == 1, step == 0)
    second = both(e == 1, step == 2)
    aide = both(both(odd == 1, later), jnp.logical_or(step == 0, step == 2))
    last = d == shards - 1
    leader = jnp.where(last, 1, 3)

    barrier = pltpu.get_barrier_semaphore()

    def greet(shard, group):
        pl.semaphore_signal(barrier, inc=1, device_id=(shard, group), device_id_type=MESH)

    @pl.when(chief)
    def _():
        each(0, shards, lambda k: [greet(lax.rem(d + k, shards), g) for g in range(2, groups)])

    @pl.when(jnp.logical_or(second, aide))
    def _():
        greet(d, e - 1)
        each(1, shards, lambda k: [greet(lax.rem(d + k, shards), e - g) for g in range(2)])

    @pl.when(e == 0)
    def _():
        greet(d, leader)

    @pl.when(both(e != 0, e != 2))
    def _():
        greet(d, 2)

    greeters = (
        jnp.where(first, eights, 3 * eights)
        - jnp.logical_or(second, aide).astype(jnp.int32)
        + jnp.where(e == 2, groups - 2, jnp.where(e == leader, 1, 0)))

    @pl.when(greeters > 0)
    def _():
        pl.semaphore_wait(barrier, greeters)

    source = odd * shards + d

    def send(src, dst, shard, group, sems, arrival=1):
        @pl.when(jnp.logical_or(d != shard, e != group))
        def _():
            pltpu.make_async_remote_copy(
                src_ref=src, dst_ref=dst, send_sem=sems.at[0], recv_sem=sems.at[arrival],
                device_id=(shard, group), device_id_type=MESH).start()

    def send_first(i):
        send(grads_in.at[i], whole_in.at[source], EIGHT * i + 2, 1, grad_sems)

    def send_wide(i, arrival):
        send(grads_in.at[i], wide_in.at[(e - 2) * shards + d], EIGHT * i, 1, wide_sems, arrival)

    def send_slim(i):
        send(grads_in.at[i, pl.ds(0, SPAN)], slim_in.at[source], EIGHT * i, 2 * pair + 1, slim_sems)
        send(grads_in.at[i, pl.ds(SPAN, SPAN)], slim_in.at[source], EIGHT * i + 2, 2 * pair + 1, slim_sems)

    @pl.when(first)
    def _():
        each(0, eights, send_first)

    @pl.when(both(later, no(last)))
    def _():
        each(0, eights, lambda i: send_wide(i, 1))

    @pl.when(both(later, last))
    def _():
        each(0, eights, lambda i: send_wide(i, 2))

    def own_first():
        return pltpu.make_async_copy(grads_in.at[eight], whole_in.at[shards + d], in_sems.at[7])

    def own_slim():
        return pltpu.make_async_copy(
            grads_in.at[eight, pl.ds(step // 2 * SPAN, SPAN)], slim_in.at[shards + d], in_sems.at[7])

    @pl.when(second)
    def _():
        own_first().start()

    @pl.when(aide)
    def _():
        own_slim().start()

    loads = [
        pltpu.make_async_copy(src, dst, in_sems.at[i])
        for i, (src, dst) in enumerate((
            (order_in, order_s), (ms_in, ms_s), (vs_in, vs_s),
            (mc_in, mc_v), (vc_in, vc_v), (master_in, master_v), (place_in, place_s),
        ))
    ]
    for load in loads:
        load.start()
    for load in loads:
        load.wait()
    m_wide[...] = mc_v[...].astype(jnp.float32)
    v_wide[...] = vc_v[...].astype(jnp.float32)

    def relay_copy(k, sem):
        return pltpu.make_async_remote_copy(
            src_ref=relay_out.at[k], dst_ref=relay_in.at[k - 1],
            send_sem=relay_sems.at[0], recv_sem=relay_sems.at[sem],
            device_id=(d, lax.rem(e + k, groups)), device_id_type=MESH)

    for k in range(groups):
        to = lax.rem(e + k, groups)
        for c in range(q):
            row = order_s[0, to * q + c]
            relay_out[k, 0, c : c + 1, :] = master_v[pl.ds(row, 1), :]
            relay_out[k, 1, c : c + 1, :] = m_wide[pl.ds(row, 1), :] * ms_s[0, row]
            relay_out[k, 2, c : c + 1, :] = v_wide[pl.ds(row, 1), :] * vs_s[0, row]

    def some(ref, count, sems):
        part = ref.at[pl.ds(0, count)]
        return pltpu.make_async_remote_copy(
            src_ref=part, dst_ref=part, send_sem=sems.at[0], recv_sem=sems.at[1],
            device_id=(d, lax.rem(e + 1, groups)), device_id_type=MESH)

    to_leader = lax.rem(leader - 2 + groups, groups)

    @pl.when(e == 2)
    def _():
        relay_copy(to_leader, 3).start()

    @pl.when(both(later, no(last)))
    def _():
        some(wide_in, eights, wide_sems).wait_send()

    @pl.when(later)
    def _():
        each(0, eights, send_slim)

    @pl.when(e == leader)
    def _():
        relay_copy(to_leader, 3).wait_recv()
        for k in range(1, groups):
            relay_copy(k, 2).start()

    @pl.when(e != leader)
    def _():
        relay_copy(1, 2).wait_recv()
        for k in range(1, groups):
            @pl.when(jnp.logical_or(e != 2, k != to_leader))
            def _():
                relay_copy(k, 1).start()

    def total(arrived, begin, count):
        if count <= UNROLL:
            gradient = arrived[begin].astype(jnp.float32)
            for k in range(1, count):
                gradient = gradient + arrived[begin + k].astype(jnp.float32)
            return gradient
        return lax.fori_loop(
            0, count, lambda k, g: g + arrived[begin + k].astype(jnp.float32),
            jnp.zeros(arrived.shape[1:], jnp.float32))

    def fold(gradient):
        return jnp.sum((gradient * gradient).reshape(-1, SUBLANES, block), axis=0)

    def send_square(shard, group, out, to, sems):
        pltpu.make_async_remote_copy(
            src_ref=out, dst_ref=to, send_sem=sems.at[0], recv_sem=sems.at[1],
            device_id=(shard, group), device_id_type=MESH).start()

    def send_second(shard, group):
        send_square(shard, group, square_out, second_in.at[eight], second_sems)

    def send_chief(shard, group):
        send_square(shard, group, square_out if group < 2 else mixed_out, square_in.at[eight], square_sems)

    def send_far(at, shard, group):
        pltpu.make_async_remote_copy(
            src_ref=far_out.at[at], dst_ref=far_in.at[0],
            send_sem=far_sems.at[0], recv_sem=far_sems.at[1],
            device_id=(shard, group), device_id_type=MESH).start()

    def row(k):
        return lax.rem(base + k, shards)

    @pl.when(second)
    def _():
        own_first().wait()
        some(whole_in, 2 * shards - 1, grad_sems).wait_recv()
        squares = jnp.zeros((SUBLANES, block), jnp.float32)
        for g in range(2):
            gradient = total(whole_in, g * shards, shards)
            squares = squares + fold(gradient)
            far_out[pl.ds(g * EIGHT, EIGHT)] = gradient
        squares = jnp.sum(squares, axis=0, keepdims=True)
        square_out[...] = squares
        second_in[eight] = squares
        for k in range(EIGHT):
            for g in range(2):
                if k != 2 or g != 1:
                    send_second(base + k, g)
        for k in range(EIGHT):
            for g in range(2):
                if k != 2 or g != 1:
                    send_far(g * EIGHT + k, base + k, g)
        each(EIGHT, shards, lambda k: [send_second(row(k), g) for g in range(2)])

    @pl.when(chief)
    def _():
        some(wide_in, (groups - 2) * (shards - 1), wide_sems).wait_recv()
        for g in range(groups - 2):
            wide_sum[g] = total(wide_in, g * shards, shards - 1)
        pltpu.make_async_remote_copy(
            src_ref=wide_in.at[pl.ds(0, groups - 2)], dst_ref=wide_in.at[pl.ds(0, groups - 2)],
            send_sem=wide_sems.at[0], recv_sem=wide_sems.at[2],
            device_id=(base, 0), device_id_type=MESH).wait_recv()
        squares = jnp.zeros((SUBLANES, block), jnp.float32)
        for g in range(groups - 2):
            squares = squares + fold(wide_sum[g] + wide_in[g * shards + shards - 1].astype(jnp.float32))
        squares = jnp.sum(squares, axis=0, keepdims=True)
        square_out[...] = squares
        square_in[eight] = squares
        send_chief(d, 0)
        some(second_in, eights, second_sems).wait_recv()
        mixed_out[...] = square_out[...] + second_in[eight]
        for k in reversed(range(EIGHT)):
            for g in reversed(range(groups)):
                if k or g > 1:
                    send_chief(base + k, g)
        each(EIGHT, shards, lambda k: [send_chief(row(k), g) for g in range(groups)])

    @pl.when(aide)
    def _():
        own_slim().wait()
        some(slim_in, 2 * shards - 1, slim_sems).wait_recv()
        for g in range(2):
            far_out[pl.ds(g * SPAN, SPAN)] = total(slim_in, g * shards, shards)
        for j in reversed(range(SPAN)):
            for g in range(2):
                owner = base + step // 2 * SPAN + j

                @pl.when(jnp.logical_or(owner != d, g != 1))
                def _():
                    send_far(g * SPAN + j, owner, e - 1 + g)

    relay_whole = some(relay_in, groups - 1, relay_sems)

    some(relay_in, groups - 2, relay_sems).wait_recv()
    rows = lax.broadcasted_iota(jnp.int32, (blocks, block), 0)
    placed = [jnp.zeros((blocks, block), jnp.float32) for _ in range(3)]
    for k in range(groups):
        frm = lax.rem(e - k + groups, groups)
        for c in range(q):
            here = rows == place_s[0, frm * q + c]
            for i in range(3):
                row = relay_out[0, i, c : c + 1, :] if k == 0 else relay_in[k - 1, i, c : c + 1, :]
                placed[i] = jnp.where(here, jnp.broadcast_to(row, (blocks, block)), placed[i])
    for i in range(3):
        state_out[i + 1] = placed[i]

    keeps = both(aide, step == 0)

    @pl.when(second)
    def _():
        state_out[0] = far_out[EIGHT + 2]

    @pl.when(keeps)
    def _():
        state_out[0] = far_out[SPAN]

    @pl.when(no(jnp.logical_or(second, keeps)))
    def _():
        some(far_in, 1, far_sems).wait_recv()
        state_out[0] = far_in[0]

    if eights > 1:
        @pl.when(chief)
        def _():
            some(square_in, eights - 1, square_sems).wait_recv()

        @pl.when(second)
        def _():
            some(second_in, eights - 1, second_sems).wait_recv()

    @pl.when(no(chief))
    def _():
        some(square_in, eights, square_sems).wait_recv()

    @pl.when(both(first, no(jnp.logical_or(chief, second))))
    def _():
        some(second_in, eights, second_sems).wait_recv()

    @pl.when(first)
    def _():
        lanes_out[...] = jnp.sum(square_in[...], axis=0) + jnp.sum(second_in[...], axis=0)

    @pl.when(later)
    def _():
        lanes_out[...] = jnp.sum(square_in[...], axis=0)

    relay_whole.wait_send()

    if eights > 1:
        @pl.when(second)
        def _():
            some(whole_in, eights - 1, grad_sems).wait_send()

    @pl.when(both(first, no(second)))
    def _():
        some(whole_in, eights, grad_sems).wait_send()

    @pl.when(both(later, last))
    def _():
        some(wide_in, eights, wide_sems).wait_send()

    @pl.when(both(later, no(aide)))
    def _():
        some(slim_in, 2 * eights, slim_sems).wait_send()

    @pl.when(aide)
    def _():
        some(slim_in, 2 * eights - 1, slim_sems).wait_send()

    @pl.when(keeps)
    def _():
        some(far_out, 2 * SPAN - 1, far_sems).wait_send()

    @pl.when(both(aide, step == 2))
    def _():
        some(far_out, 2 * SPAN, far_sems).wait_send()

    @pl.when(second)
    def _():
        some(square_all, 2 * shards - 1, second_sems).wait_send()
        some(far_out, 2 * EIGHT - 1, far_sems).wait_send()

    @pl.when(chief)
    def _():
        some(square_all, shards * groups - 1, square_sems).wait_send()


def update(count, state, lanes, master_out, mc_out, ms_out, vc_out, vs_out):
    gradient, master, moment_one, moment_two = (state[i] for i in range(4))
    blocks, block = gradient.shape

    total_squares = jnp.sum(lanes[...], axis=1, keepdims=True)
    root_mean = jnp.sqrt(total_squares / count + NORM_EPS)
    clip_factor = jnp.minimum(1.0, CLIP_RMS / root_mean)

    clipped = clip_factor * gradient
    m_next = BETA_ONE * moment_one + (1.0 - BETA_ONE) * clipped
    v_next = BETA_TWO * moment_two + (1.0 - BETA_TWO) * clipped * clipped
    bias_one = 1.0 - BETA_ONE**STEP
    bias_two = 1.0 - BETA_TWO**STEP
    m_mag = jnp.max(jnp.abs(m_next), axis=1, keepdims=True) + QUANT_EPS
    v_mag = jnp.max(jnp.abs(v_next), axis=1, keepdims=True) + QUANT_EPS
    step = m_next / bias_one / (jnp.sqrt(v_next / bias_two) + ADAM_EPS)
    master_out[...] = master - LEARN_RATE * (step + DECAY_RATE * master)
    mc_out[...] = (m_next / m_mag).astype(jnp.bfloat16)
    vc_out[...] = (v_next / v_mag).astype(jnp.bfloat16)
    rows = lax.broadcasted_iota(jnp.int32, (blocks, block), 0)
    diagonal = rows == lax.broadcasted_iota(jnp.int32, (blocks, block), 1)
    ms_out[...] = jnp.sum(jnp.where(diagonal, m_mag, 0.0), axis=0, keepdims=True)[:, :blocks]
    vs_out[...] = jnp.sum(jnp.where(diagonal, v_mag, 0.0), axis=0, keepdims=True)[:, :blocks]


def body(shards, groups, master_old, m_codes, m_scale, v_codes, v_scale, grad_parts, send_order, recv_place):
    blocks, block = master_old.shape[2:]
    eights = shards // EIGHT
    f32, bf16 = jnp.float32, jnp.bfloat16
    wide = (blocks, block)
    anywhere = pl.BlockSpec(memory_space=pl.ANY)
    vmem = pl.BlockSpec(memory_space=pltpu.VMEM)
    state, lanes = pl.pallas_call(
        functools.partial(kernel, shards, groups),
        out_shape=(pltpu.VMEM((4, blocks, block), f32), pltpu.VMEM((1, block), f32)),
        in_specs=[anywhere] * 8,
        out_specs=(vmem, vmem),
        scratch_shapes=[
            pltpu.VMEM(wide, f32),
            pltpu.VMEM(wide, bf16),
            pltpu.VMEM(wide, bf16),
            pltpu.VMEM(wide, f32),
            pltpu.VMEM(wide, f32),
            pltpu.SMEM((1, blocks), f32),
            pltpu.SMEM((1, blocks), f32),
            pltpu.SMEM((1, blocks), jnp.int32),
            pltpu.SMEM((1, blocks), jnp.int32),
            pltpu.VMEM((groups, 3, blocks // groups, block), f32),
            pltpu.VMEM((groups - 1, 3, blocks // groups, block), f32),
            pltpu.VMEM((2 * shards, EIGHT, blocks, block), bf16),
            pltpu.VMEM(((groups - 2) * shards, EIGHT, blocks, block), bf16),
            pltpu.VMEM((2 * shards, SPAN, blocks, block), bf16),
            pltpu.VMEM((2 * EIGHT, blocks, block), f32),
            pltpu.VMEM((1, blocks, block), f32),
            pltpu.VMEM((groups - 2, EIGHT, blocks, block), f32),
            pltpu.VMEM((1, block), f32),
            pltpu.VMEM((1, block), f32),
            pltpu.VMEM((eights, 1, block), f32),
            pltpu.VMEM((eights, 1, block), f32),
            pltpu.VMEM((shards * groups - 1, 1, block), f32),
            pltpu.SemaphoreType.DMA((8,)),
            pltpu.SemaphoreType.DMA((2,)),
            pltpu.SemaphoreType.DMA((2,)),
            pltpu.SemaphoreType.DMA((3,)),
            pltpu.SemaphoreType.DMA((4,)),
            pltpu.SemaphoreType.DMA((2,)),
            pltpu.SemaphoreType.DMA((2,)),
            pltpu.SemaphoreType.DMA((2,)),
        ],
        compiler_params=pltpu.CompilerParams(collective_id=0, has_side_effects=True),
    )(
        master_old.reshape(wide), m_codes.reshape(wide), m_scale.reshape(1, blocks),
        v_codes.reshape(wide), v_scale.reshape(1, blocks),
        grad_parts.reshape(eights, EIGHT, blocks, block),
        send_order.reshape(1, blocks), recv_place.reshape(1, blocks),
    )
    master_new, mc, ms, vc, vs = pl.pallas_call(
        functools.partial(update, shards * groups * blocks * block),
        out_shape=(
            jax.ShapeDtypeStruct(wide, f32),
            jax.ShapeDtypeStruct(wide, bf16),
            jax.ShapeDtypeStruct((1, blocks), f32),
            jax.ShapeDtypeStruct(wide, bf16),
            jax.ShapeDtypeStruct((1, blocks), f32),
        ),
        in_specs=[vmem, vmem],
        out_specs=(vmem,) * 5,
    )(
        pltpu.with_memory_space_constraint(state, pltpu.VMEM),
        pltpu.with_memory_space_constraint(lanes, pltpu.VMEM))
    return master_new[None], mc[None], ms, vc[None], vs


def solution(mesh):
    rows = P("dp", "expert", None, None)
    flat = P("dp", "expert", None)
    return jax.shard_map(
        functools.partial(body, mesh.shape["dp"], mesh.shape["expert"]),
        mesh=mesh,
        in_specs=(rows, rows, flat, rows, flat, rows, flat, flat),
        out_specs=(
            P("expert", "dp", None),
            P("expert", "dp", None),
            P("expert", "dp"),
            P("expert", "dp", None),
            P("expert", "dp"),
        ),
        check_vma=False,
    )
```

```python
import functools

import jax
import jax.numpy as jnp
from jax import lax
from jax.experimental import pallas as pl
from jax.experimental.pallas import tpu as pltpu
from jax.sharding import PartitionSpec as P

STEP = 200

BETA_ONE = 0.9
BETA_TWO = 0.999
ADAM_EPS = 1e-08
LEARN_RATE = 0.05
DECAY_RATE = 0.1
CLIP_RMS = 1.0
QUANT_EPS = 1e-06
NORM_EPS = 1e-06

MESH = pl.DeviceIdType.MESH
UNROLL = 40
SUBLANES = 8
EIGHT = 8
SPAN = EIGHT // 2


def each(first, last, step):
    if last - first <= UNROLL:
        for k in range(first, last):
            step(k)
    else:
        lax.fori_loop(first, last, lambda k, c: (step(k), c)[1], 0)


def kernel(
    shards, groups,
    master_in, mc_in, ms_in, vc_in, vs_in, grads_in, order_in, place_in,
    state_out, lanes_out,
    master_v, mc_v, vc_v, m_wide, v_wide,
    ms_s, vs_s, order_s, place_s,
    relay_out, relay_in, whole_in, wide_in, slim_in, far_out, far_in,
    wide_sum, square_out, mixed_out, square_in, second_in, square_all,
    in_sems, grad_sems, slim_sems, wide_sems, relay_sems, far_sems, square_sems, second_sems,
):
    d = lax.axis_index("dp")
    e = lax.axis_index("expert")
    blocks, block = master_v.shape
    q = blocks // groups
    eights = shards // EIGHT
    odd = lax.rem(e, 2)
    pair = e // 2
    eight = d // EIGHT
    step = lax.rem(d, EIGHT)
    base = EIGHT * eight
    both = jnp.logical_and
    no = jnp.logical_not
    first = e < 2
    later = e >= 2
    chief = both(e == 1, step == 0)
    second = both(e == 1, step == 2)
    aide = both(both(odd == 1, later), jnp.logical_or(step == 0, step == 2))
    last = d == shards - 1
    leader = jnp.where(last, 1, 3)

    barrier = pltpu.get_barrier_semaphore()

    def greet(shard, group):
        pl.semaphore_signal(barrier, inc=1, device_id=(shard, group), device_id_type=MESH)

    @pl.when(chief)
    def _():
        each(0, shards, lambda k: [greet(lax.rem(d + k, shards), g) for g in range(2, groups)])

    @pl.when(jnp.logical_or(second, aide))
    def _():
        greet(d, e - 1)
        each(1, shards, lambda k: [greet(lax.rem(d + k, shards), e - g) for g in range(2)])

    @pl.when(e == 0)
    def _():
        greet(d, leader)

    @pl.when(both(e != 0, e != 2))
    def _():
        greet(d, 2)

    greeters = (
        jnp.where(first, eights, 3 * eights)
        - jnp.logical_or(second, aide).astype(jnp.int32)
        + jnp.where(e == 2, groups - 2, jnp.where(e == leader, 1, 0)))

    @pl.when(greeters > 0)
    def _():
        pl.semaphore_wait(barrier, greeters)

    source = odd * shards + d

    def send(src, dst, shard, group, sems, arrival=1):
        @pl.when(jnp.logical_or(d != shard, e != group))
        def _():
            pltpu.make_async_remote_copy(
                src_ref=src, dst_ref=dst, send_sem=sems.at[0], recv_sem=sems.at[arrival],
                device_id=(shard, group), device_id_type=MESH).start()

    def send_first(i):
        send(grads_in.at[i], whole_in.at[source], EIGHT * i + 2, 1, grad_sems)

    def send_wide(i, arrival):
        send(grads_in.at[i], wide_in.at[(e - 2) * shards + d], EIGHT * i, 1, wide_sems, arrival)

    def send_slim(i):
        send(grads_in.at[i, pl.ds(0, SPAN)], slim_in.at[source], EIGHT * i, 2 * pair + 1, slim_sems)
        send(grads_in.at[i, pl.ds(SPAN, SPAN)], slim_in.at[source], EIGHT * i + 2, 2 * pair + 1, slim_sems)

    @pl.when(first)
    def _():
        each(0, eights, send_first)

    @pl.when(both(later, no(last)))
    def _():
        each(0, eights, lambda i: send_wide(i, 1))

    @pl.when(both(later, last))
    def _():
        @pl.when(odd == 1)
        def _():
            each(0, eights, lambda i: send_wide(i, 2))

        @pl.when(odd == 0)
        def _():
            each(0, eights, lambda i: send_wide(i, 3))

    def own_first():
        return pltpu.make_async_copy(grads_in.at[eight], whole_in.at[shards + d], in_sems.at[7])

    def own_slim():
        return pltpu.make_async_copy(
            grads_in.at[eight, pl.ds(step // 2 * SPAN, SPAN)], slim_in.at[shards + d], in_sems.at[7])

    @pl.when(second)
    def _():
        own_first().start()

    @pl.when(aide)
    def _():
        own_slim().start()

    loads = [
        pltpu.make_async_copy(src, dst, in_sems.at[i])
        for i, (src, dst) in enumerate((
            (order_in, order_s), (ms_in, ms_s), (vs_in, vs_s),
            (mc_in, mc_v), (vc_in, vc_v), (master_in, master_v), (place_in, place_s),
        ))
    ]
    for load in loads:
        load.start()
    for load in loads:
        load.wait()
    m_wide[...] = mc_v[...].astype(jnp.float32)
    v_wide[...] = vc_v[...].astype(jnp.float32)

    def relay_copy(k, sem):
        return pltpu.make_async_remote_copy(
            src_ref=relay_out.at[k], dst_ref=relay_in.at[k - 1],
            send_sem=relay_sems.at[0], recv_sem=relay_sems.at[sem],
            device_id=(d, lax.rem(e + k, groups)), device_id_type=MESH)

    for k in range(groups):
        to = lax.rem(e + k, groups)
        for c in range(q):
            row = order_s[0, to * q + c]
            relay_out[k, 0, c : c + 1, :] = master_v[pl.ds(row, 1), :]
            relay_out[k, 1, c : c + 1, :] = m_wide[pl.ds(row, 1), :] * ms_s[0, row]
            relay_out[k, 2, c : c + 1, :] = v_wide[pl.ds(row, 1), :] * vs_s[0, row]

    def some(ref, count, sems):
        part = ref.at[pl.ds(0, count)]
        return pltpu.make_async_remote_copy(
            src_ref=part, dst_ref=part, send_sem=sems.at[0], recv_sem=sems.at[1],
            device_id=(d, lax.rem(e + 1, groups)), device_id_type=MESH)

    to_leader = lax.rem(leader - 2 + groups, groups)

    @pl.when(e == 2)
    def _():
        relay_copy(to_leader, 3).start()

    @pl.when(both(later, no(both(last, odd == 0))))
    def _():
        some(wide_in, eights, wide_sems).wait_send()

    @pl.when(later)
    def _():
        each(0, eights, send_slim)

    @pl.when(e == leader)
    def _():
        relay_copy(to_leader, 3).wait_recv()
        for k in range(1, groups):
            relay_copy(k, 2).start()

    @pl.when(e != leader)
    def _():
        relay_copy(1, 2).wait_recv()
        for k in range(1, groups):
            @pl.when(jnp.logical_or(e != 2, k != to_leader))
            def _():
                relay_copy(k, 1).start()

    def total(arrived, begin, count):
        if count <= UNROLL:
            gradient = arrived[begin].astype(jnp.float32)
            for k in range(1, count):
                gradient = gradient + arrived[begin + k].astype(jnp.float32)
            return gradient
        return lax.fori_loop(
            0, count, lambda k, g: g + arrived[begin + k].astype(jnp.float32),
            jnp.zeros(arrived.shape[1:], jnp.float32))

    def fold(gradient):
        return jnp.sum((gradient * gradient).reshape(-1, SUBLANES, block), axis=0)

    def send_square(shard, group, out, to, sems):
        pltpu.make_async_remote_copy(
            src_ref=out, dst_ref=to, send_sem=sems.at[0], recv_sem=sems.at[1],
            device_id=(shard, group), device_id_type=MESH).start()

    def send_second(shard, group):
        send_square(shard, group, square_out, second_in.at[eight], second_sems)

    def send_chief(shard, group):
        send_square(shard, group, square_out if group < 2 else mixed_out, square_in.at[eight], square_sems)

    def send_far(at, shard, group):
        pltpu.make_async_remote_copy(
            src_ref=far_out.at[at], dst_ref=far_in.at[0],
            send_sem=far_sems.at[0], recv_sem=far_sems.at[1],
            device_id=(shard, group), device_id_type=MESH).start()

    def row(k):
        return lax.rem(base + k, shards)

    @pl.when(second)
    def _():
        own_first().wait()
        some(whole_in, 2 * shards - 1, grad_sems).wait_recv()
        squares = jnp.zeros((SUBLANES, block), jnp.float32)
        for g in range(2):
            gradient = total(whole_in, g * shards, shards)
            squares = squares + fold(gradient)
            far_out[pl.ds(g * EIGHT, EIGHT)] = gradient
        squares = jnp.sum(squares, axis=0, keepdims=True)
        square_out[...] = squares
        second_in[eight] = squares
        for k in range(EIGHT):
            for g in range(2):
                if k != 2 or g != 1:
                    send_second(base + k, g)
        for k in range(EIGHT):
            for g in range(2):
                if k != 2 or g != 1:
                    send_far(g * EIGHT + k, base + k, g)
        each(EIGHT, shards, lambda k: [send_second(row(k), g) for g in range(2)])

    @pl.when(chief)
    def _():
        some(wide_in, (groups - 2) * (shards - 1), wide_sems).wait_recv()
        for g in range(groups - 2):
            wide_sum[g] = total(wide_in, g * shards, shards - 1)
        squares = jnp.zeros((SUBLANES, block), jnp.float32)
        half = wide_in.at[pl.ds(0, groups // 2 - 1)]
        for parity in (1, 0):
            pltpu.make_async_remote_copy(
                src_ref=half, dst_ref=half, send_sem=wide_sems.at[0], recv_sem=wide_sems.at[3 - parity],
                device_id=(base, 0), device_id_type=MESH).wait_recv()
            for g in range(parity, groups - 2, 2):
                squares = squares + fold(wide_sum[g] + wide_in[g * shards + shards - 1].astype(jnp.float32))
        squares = jnp.sum(squares, axis=0, keepdims=True)
        square_out[...] = squares
        square_in[eight] = squares
        send_chief(d, 0)
        for k in reversed(range(1, EIGHT)):
            send_chief(base + k, 1)
            pl.when(base + k != shards - 1)(lambda: send_chief(base + k, 0))
        some(second_in, eights, second_sems).wait_recv()
        mixed_out[...] = square_out[...] + second_in[eight]
        pl.when(base + EIGHT == shards)(lambda: send_chief(shards - 1, 0))
        for k in reversed(range(EIGHT)):
            for g in reversed(range(2, groups)):
                send_chief(base + k, g)
        each(EIGHT, shards, lambda k: [send_chief(row(k), g) for g in range(groups)])

    @pl.when(aide)
    def _():
        own_slim().wait()
        some(slim_in, 2 * shards - 1, slim_sems).wait_recv()
        for g in range(2):
            far_out[pl.ds(g * SPAN, SPAN)] = total(slim_in, g * shards, shards)
        for j in reversed(range(SPAN)):
            for g in range(2):
                owner = base + step // 2 * SPAN + j

                @pl.when(jnp.logical_or(owner != d, g != 1))
                def _():
                    send_far(g * SPAN + j, owner, e - 1 + g)

    relay_whole = some(relay_in, groups - 1, relay_sems)

    some(relay_in, groups - 2, relay_sems).wait_recv()
    rows = lax.broadcasted_iota(jnp.int32, (blocks, block), 0)
    placed = [jnp.zeros((blocks, block), jnp.float32) for _ in range(3)]
    for k in range(groups):
        frm = lax.rem(e - k + groups, groups)
        for c in range(q):
            here = rows == place_s[0, frm * q + c]
            for i in range(3):
                row = relay_out[0, i, c : c + 1, :] if k == 0 else relay_in[k - 1, i, c : c + 1, :]
                placed[i] = jnp.where(here, jnp.broadcast_to(row, (blocks, block)), placed[i])
    for i in range(3):
        state_out[i + 1] = placed[i]

    keeps = both(aide, step == 0)

    @pl.when(second)
    def _():
        state_out[0] = far_out[EIGHT + 2]

    @pl.when(keeps)
    def _():
        state_out[0] = far_out[SPAN]

    @pl.when(no(jnp.logical_or(second, keeps)))
    def _():
        some(far_in, 1, far_sems).wait_recv()
        state_out[0] = far_in[0]

    if eights > 1:
        @pl.when(chief)
        def _():
            some(square_in, eights - 1, square_sems).wait_recv()

        @pl.when(second)
        def _():
            some(second_in, eights - 1, second_sems).wait_recv()

    @pl.when(no(chief))
    def _():
        some(square_in, eights, square_sems).wait_recv()

    @pl.when(both(first, no(jnp.logical_or(chief, second))))
    def _():
        some(second_in, eights, second_sems).wait_recv()

    @pl.when(first)
    def _():
        lanes_out[...] = jnp.sum(square_in[...], axis=0) + jnp.sum(second_in[...], axis=0)

    @pl.when(later)
    def _():
        lanes_out[...] = jnp.sum(square_in[...], axis=0)

    relay_whole.wait_send()

    if eights > 1:
        @pl.when(second)
        def _():
            some(whole_in, eights - 1, grad_sems).wait_send()

    @pl.when(both(first, no(second)))
    def _():
        some(whole_in, eights, grad_sems).wait_send()

    @pl.when(both(later, both(last, odd == 0)))
    def _():
        some(wide_in, eights, wide_sems).wait_send()

    @pl.when(both(later, no(aide)))
    def _():
        some(slim_in, 2 * eights, slim_sems).wait_send()

    @pl.when(aide)
    def _():
        some(slim_in, 2 * eights - 1, slim_sems).wait_send()

    @pl.when(keeps)
    def _():
        some(far_out, 2 * SPAN - 1, far_sems).wait_send()

    @pl.when(both(aide, step == 2))
    def _():
        some(far_out, 2 * SPAN, far_sems).wait_send()

    @pl.when(second)
    def _():
        some(square_all, 2 * shards - 1, second_sems).wait_send()
        some(far_out, 2 * EIGHT - 1, far_sems).wait_send()

    @pl.when(chief)
    def _():
        some(square_all, shards * groups - 1, square_sems).wait_send()


def update(count, state, lanes, master_out, mc_out, ms_out, vc_out, vs_out):
    gradient, master, moment_one, moment_two = (state[i] for i in range(4))
    blocks, block = gradient.shape

    total_squares = jnp.sum(lanes[...], axis=1, keepdims=True)
    root_mean = jnp.sqrt(total_squares / count + NORM_EPS)
    clip_factor = jnp.minimum(1.0, CLIP_RMS / root_mean)

    clipped = clip_factor * gradient
    m_next = BETA_ONE * moment_one + (1.0 - BETA_ONE) * clipped
    v_next = BETA_TWO * moment_two + (1.0 - BETA_TWO) * clipped * clipped
    bias_one = 1.0 - BETA_ONE**STEP
    bias_two = 1.0 - BETA_TWO**STEP
    m_mag = jnp.max(jnp.abs(m_next), axis=1, keepdims=True) + QUANT_EPS
    v_mag = jnp.max(jnp.abs(v_next), axis=1, keepdims=True) + QUANT_EPS
    step = m_next / bias_one / (jnp.sqrt(v_next / bias_two) + ADAM_EPS)
    master_out[...] = master - LEARN_RATE * (step + DECAY_RATE * master)
    mc_out[...] = (m_next / m_mag).astype(jnp.bfloat16)
    vc_out[...] = (v_next / v_mag).astype(jnp.bfloat16)
    rows = lax.broadcasted_iota(jnp.int32, (blocks, block), 0)
    diagonal = rows == lax.broadcasted_iota(jnp.int32, (blocks, block), 1)
    ms_out[...] = jnp.sum(jnp.where(diagonal, m_mag, 0.0), axis=0, keepdims=True)[:, :blocks]
    vs_out[...] = jnp.sum(jnp.where(diagonal, v_mag, 0.0), axis=0, keepdims=True)[:, :blocks]


def body(shards, groups, master_old, m_codes, m_scale, v_codes, v_scale, grad_parts, send_order, recv_place):
    blocks, block = master_old.shape[2:]
    eights = shards // EIGHT
    f32, bf16 = jnp.float32, jnp.bfloat16
    wide = (blocks, block)
    anywhere = pl.BlockSpec(memory_space=pl.ANY)
    vmem = pl.BlockSpec(memory_space=pltpu.VMEM)
    state, lanes = pl.pallas_call(
        functools.partial(kernel, shards, groups),
        out_shape=(pltpu.VMEM((4, blocks, block), f32), pltpu.VMEM((1, block), f32)),
        in_specs=[anywhere] * 8,
        out_specs=(vmem, vmem),
        scratch_shapes=[
            pltpu.VMEM(wide, f32),
            pltpu.VMEM(wide, bf16),
            pltpu.VMEM(wide, bf16),
            pltpu.VMEM(wide, f32),
            pltpu.VMEM(wide, f32),
            pltpu.SMEM((1, blocks), f32),
            pltpu.SMEM((1, blocks), f32),
            pltpu.SMEM((1, blocks), jnp.int32),
            pltpu.SMEM((1, blocks), jnp.int32),
            pltpu.VMEM((groups, 3, blocks // groups, block), f32),
            pltpu.VMEM((groups - 1, 3, blocks // groups, block), f32),
            pltpu.VMEM((2 * shards, EIGHT, blocks, block), bf16),
            pltpu.VMEM(((groups - 2) * shards, EIGHT, blocks, block), bf16),
            pltpu.VMEM((2 * shards, SPAN, blocks, block), bf16),
            pltpu.VMEM((2 * EIGHT, blocks, block), f32),
            pltpu.VMEM((1, blocks, block), f32),
            pltpu.VMEM((groups - 2, EIGHT, blocks, block), f32),
            pltpu.VMEM((1, block), f32),
            pltpu.VMEM((1, block), f32),
            pltpu.VMEM((eights, 1, block), f32),
            pltpu.VMEM((eights, 1, block), f32),
            pltpu.VMEM((shards * groups - 1, 1, block), f32),
            pltpu.SemaphoreType.DMA((8,)),
            pltpu.SemaphoreType.DMA((2,)),
            pltpu.SemaphoreType.DMA((2,)),
            pltpu.SemaphoreType.DMA((4,)),
            pltpu.SemaphoreType.DMA((4,)),
            pltpu.SemaphoreType.DMA((2,)),
            pltpu.SemaphoreType.DMA((2,)),
            pltpu.SemaphoreType.DMA((2,)),
        ],
        compiler_params=pltpu.CompilerParams(collective_id=0, has_side_effects=True),
    )(
        master_old.reshape(wide), m_codes.reshape(wide), m_scale.reshape(1, blocks),
        v_codes.reshape(wide), v_scale.reshape(1, blocks),
        grad_parts.reshape(eights, EIGHT, blocks, block),
        send_order.reshape(1, blocks), recv_place.reshape(1, blocks),
    )
    master_new, mc, ms, vc, vs = pl.pallas_call(
        functools.partial(update, shards * groups * blocks * block),
        out_shape=(
            jax.ShapeDtypeStruct(wide, f32),
            jax.ShapeDtypeStruct(wide, bf16),
            jax.ShapeDtypeStruct((1, blocks), f32),
            jax.ShapeDtypeStruct(wide, bf16),
            jax.ShapeDtypeStruct((1, blocks), f32),
        ),
        in_specs=[vmem, vmem],
        out_specs=(vmem,) * 5,
    )(
        pltpu.with_memory_space_constraint(state, pltpu.VMEM),
        pltpu.with_memory_space_constraint(lanes, pltpu.VMEM))
    return master_new[None], mc[None], ms, vc[None], vs


def solution(mesh):
    rows = P("dp", "expert", None, None)
    flat = P("dp", "expert", None)
    return jax.shard_map(
        functools.partial(body, mesh.shape["dp"], mesh.shape["expert"]),
        mesh=mesh,
        in_specs=(rows, rows, flat, rows, flat, rows, flat, flat),
        out_specs=(
            P("expert", "dp", None),
            P("expert", "dp", None),
            P("expert", "dp"),
            P("expert", "dp", None),
            P("expert", "dp"),
        ),
        check_vma=False,
    )
```

```python
import functools

import jax
import jax.numpy as jnp
from jax import lax
from jax.experimental import pallas as pl
from jax.experimental.pallas import tpu as pltpu
from jax.sharding import PartitionSpec as P

STEP = 200

BETA_ONE = 0.9
BETA_TWO = 0.999
ADAM_EPS = 1e-08
LEARN_RATE = 0.05
DECAY_RATE = 0.1
CLIP_RMS = 1.0
QUANT_EPS = 1e-06
NORM_EPS = 1e-06

MESH = pl.DeviceIdType.MESH
UNROLL = 40
SUBLANES = 8
EIGHT = 8
SPAN = EIGHT // 2


def each(first, last, step):
    if last - first <= UNROLL:
        for k in range(first, last):
            step(k)
    else:
        lax.fori_loop(first, last, lambda k, c: (step(k), c)[1], 0)


def kernel(
    shards, groups,
    master_in, mc_in, ms_in, vc_in, vs_in, grads_in, order_in, place_in,
    state_out, lanes_out,
    master_v, mc_v, vc_v, m_wide, v_wide,
    ms_s, vs_s, order_s, place_s,
    relay_out, relay_in, whole_in, wide_in, slim_in, far_out, far_in,
    wide_sum, square_out, mixed_out, square_in, second_in, square_all,
    in_sems, grad_sems, slim_sems, wide_sems, relay_sems, far_sems, square_sems, second_sems,
):
    d = lax.axis_index("dp")
    e = lax.axis_index("expert")
    blocks, block = master_v.shape
    q = blocks // groups
    eights = shards // EIGHT
    odd = lax.rem(e, 2)
    pair = lax.div(e, 2)
    eight = lax.div(d, EIGHT)
    step = lax.rem(d, EIGHT)
    base = EIGHT * eight
    both = jnp.logical_and
    no = jnp.logical_not
    first = e < 2
    later = e >= 2
    chief = both(e == 1, step == 0)
    second = both(e == 1, step == 2)
    aide = both(both(odd == 1, later), jnp.logical_or(step == 0, step == 2))
    last = d == shards - 1
    leader = jnp.where(last, 1, 3)

    barrier = pltpu.get_barrier_semaphore()

    def greet(shard, group):
        pl.semaphore_signal(barrier, inc=1, device_id=(shard, group), device_id_type=MESH)

    @pl.when(e != 2)
    def _():
        @pl.when(chief)
        def _():
            each(0, shards, lambda k: [greet(lax.rem(d + k, shards), g) for g in range(2, groups)])

        @pl.when(jnp.logical_or(second, aide))
        def _():
            greet(d, e - 1)
            each(1, shards, lambda k: [greet(lax.rem(d + k, shards), e - g) for g in range(2)])

        @pl.when(e == 0)
        def _():
            greet(d, leader)

        @pl.when(e != 0)
        def _():
            greet(d, 2)

    greeters = (
        jnp.where(first, eights, 3 * eights)
        - jnp.logical_or(second, aide).astype(jnp.int32)
        + jnp.where(e == 2, groups - 2, jnp.where(e == leader, 1, 0)))

    @pl.when(greeters > 0)
    def _():
        pl.semaphore_wait(barrier, greeters)

    source = odd * shards + d

    def send(src, dst, shard, group, sems, arrives=1):
        @pl.when(jnp.logical_or(d != shard, e != group))
        def _():
            pltpu.make_async_remote_copy(
                src_ref=src, dst_ref=dst, send_sem=sems.at[0], recv_sem=sems.at[arrives],
                device_id=(shard, group), device_id_type=MESH).start()

    def send_first(i):
        send(grads_in.at[i], whole_in.at[source], EIGHT * i + 2, 1, grad_sems, jnp.where(last, 2, 1))

    arrival = jnp.where(last, 3 - odd, 1)

    def send_wide(i):
        pltpu.make_async_remote_copy(
            src_ref=grads_in.at[i], dst_ref=wide_in.at[(e - 2) * shards + d],
            send_sem=wide_sems.at[0], recv_sem=wide_sems.at[arrival],
            device_id=(EIGHT * i, 1), device_id_type=MESH).start()

    def send_slim(i):
        send(grads_in.at[i, pl.ds(0, SPAN)], slim_in.at[source], EIGHT * i, 2 * pair + 1, slim_sems)
        send(grads_in.at[i, pl.ds(SPAN, SPAN)], slim_in.at[source], EIGHT * i + 2, 2 * pair + 1, slim_sems)

    @pl.when(later)
    def _():
        each(0, eights, send_wide)

    @pl.when(first)
    def _():
        each(0, eights, send_first)

    def own_first():
        return pltpu.make_async_copy(grads_in.at[eight], whole_in.at[shards + d], in_sems.at[7])

    def own_slim():
        return pltpu.make_async_copy(
            grads_in.at[eight, pl.ds(lax.div(step, 2) * SPAN, SPAN)], slim_in.at[shards + d], in_sems.at[7])

    @pl.when(second)
    def _():
        own_first().start()

    @pl.when(aide)
    def _():
        own_slim().start()

    loads = [
        pltpu.make_async_copy(src, dst, in_sems.at[i])
        for i, (src, dst) in enumerate((
            (order_in, order_s), (ms_in, ms_s), (vs_in, vs_s),
            (mc_in, mc_v), (vc_in, vc_v), (master_in, master_v), (place_in, place_s),
        ))
    ]
    for load in loads:
        load.start()
    for load in loads:
        load.wait()
    m_wide[...] = mc_v[...].astype(jnp.float32)
    v_wide[...] = vc_v[...].astype(jnp.float32)

    def relay_copy(k, sem):
        return pltpu.make_async_remote_copy(
            src_ref=relay_out.at[k], dst_ref=relay_in.at[k - 1],
            send_sem=relay_sems.at[0], recv_sem=relay_sems.at[sem],
            device_id=(d, lax.rem(e + k, groups)), device_id_type=MESH)

    for k in range(groups):
        to = lax.rem(e + k, groups)
        for c in range(q):
            row = order_s[0, to * q + c]
            relay_out[k, 0, c : c + 1, :] = master_v[pl.ds(row, 1), :]
            relay_out[k, 1, c : c + 1, :] = m_wide[pl.ds(row, 1), :] * ms_s[0, row]
            relay_out[k, 2, c : c + 1, :] = v_wide[pl.ds(row, 1), :] * vs_s[0, row]

    def some(ref, count, sems):
        part = ref.at[pl.ds(0, count)]
        return pltpu.make_async_remote_copy(
            src_ref=part, dst_ref=part, send_sem=sems.at[0], recv_sem=sems.at[1],
            device_id=(d, lax.rem(e + 1, groups)), device_id_type=MESH)

    to_leader = lax.rem(leader - 2 + groups, groups)

    @pl.when(e == 2)
    def _():
        relay_copy(to_leader, 3).start()

    @pl.when(both(later, no(both(last, odd == 0))))
    def _():
        some(wide_in, eights, wide_sems).wait_send()

    @pl.when(later)
    def _():
        each(0, eights, send_slim)

    @pl.when(e == leader)
    def _():
        relay_copy(to_leader, 3).wait_recv()
        for k in range(1, groups):
            relay_copy(k, 2).start()

    @pl.when(e != leader)
    def _():
        relay_copy(1, 2).wait_recv()
        for k in range(1, groups):
            @pl.when(jnp.logical_or(e != 2, k != to_leader))
            def _():
                relay_copy(k, 1).start()

    def total(arrived, begin, count):
        if count <= UNROLL:
            gradient = arrived[begin].astype(jnp.float32)
            for k in range(1, count):
                gradient = gradient + arrived[begin + k].astype(jnp.float32)
            return gradient
        return lax.fori_loop(
            0, count, lambda k, g: g + arrived[begin + k].astype(jnp.float32),
            jnp.zeros(arrived.shape[1:], jnp.float32))

    def fold(gradient):
        return jnp.sum((gradient * gradient).reshape(-1, SUBLANES, block), axis=0)

    def send_square(shard, group, out, to, sems):
        pltpu.make_async_remote_copy(
            src_ref=out, dst_ref=to, send_sem=sems.at[0], recv_sem=sems.at[1],
            device_id=(shard, group), device_id_type=MESH).start()

    def send_second(shard, group):
        send_square(shard, group, square_out, second_in.at[eight], second_sems)

    def send_chief(shard, group):
        send_square(shard, group, square_out if group < 2 else mixed_out, square_in.at[eight], square_sems)

    def send_far(at, shard, group):
        pltpu.make_async_remote_copy(
            src_ref=far_out.at[at], dst_ref=far_in.at[0],
            send_sem=far_sems.at[0], recv_sem=far_sems.at[1],
            device_id=(shard, group), device_id_type=MESH).start()

    def row(k):
        return lax.rem(base + k, shards)

    @pl.when(second)
    def _():
        own_first().wait()
        some(whole_in, 2 * (shards - 1) - 1, grad_sems).wait_recv()
        for g in range(2):
            far_out[pl.ds(g * EIGHT, EIGHT)] = total(whole_in, g * shards, shards - 1)
        pltpu.make_async_remote_copy(
            src_ref=whole_in.at[pl.ds(0, 2)], dst_ref=whole_in.at[pl.ds(0, 2)],
            send_sem=grad_sems.at[0], recv_sem=grad_sems.at[2],
            device_id=(base, 0), device_id_type=MESH).wait_recv()
        squares = jnp.zeros((SUBLANES, block), jnp.float32)
        for g in range(2):
            gradient = far_out[pl.ds(g * EIGHT, EIGHT)] + whole_in[g * shards + shards - 1].astype(jnp.float32)
            squares = squares + fold(gradient)
            far_out[pl.ds(g * EIGHT, EIGHT)] = gradient
        squares = jnp.sum(squares, axis=0, keepdims=True)
        square_out[...] = squares
        second_in[eight] = squares
        send_second(base, 1)
        send_second(base, 0)
        for k in range(1, EIGHT):
            for g in range(2):
                if k != 2 or g != 1:
                    send_second(base + k, g)
        send_far(0, base, 0)
        send_far(EIGHT, base, 1)
        for k in range(1, EIGHT):
            for g in range(2):
                if k != 2 or g != 1:
                    send_far(g * EIGHT + k, base + k, g)
        each(EIGHT, shards, lambda k: [send_second(row(k), g) for g in range(2)])

    @pl.when(chief)
    def _():
        some(wide_in, (groups - 2) * (shards - 1), wide_sems).wait_recv()
        for g in range(groups - 2):
            wide_sum[g] = total(wide_in, g * shards, shards - 1)
        squares = jnp.zeros((SUBLANES, block), jnp.float32)
        half = wide_in.at[pl.ds(0, groups // 2 - 1)]
        for parity in (1, 0):
            pltpu.make_async_remote_copy(
                src_ref=half, dst_ref=half, send_sem=wide_sems.at[0], recv_sem=wide_sems.at[3 - parity],
                device_id=(base, 0), device_id_type=MESH).wait_recv()
            for g in range(parity, groups - 2, 2):
                squares = squares + fold(wide_sum[g] + wide_in[g * shards + shards - 1].astype(jnp.float32))
        squares = jnp.sum(squares, axis=0, keepdims=True)
        square_out[...] = squares
        square_in[eight] = squares
        send_chief(d, 0)
        for k in reversed(range(1, EIGHT)):
            send_chief(base + k, 1)
            pl.when(base + k != shards - 1)(lambda: send_chief(base + k, 0))
        some(second_in, eights, second_sems).wait_recv()
        mixed_out[...] = square_out[...] + second_in[eight]
        pl.when(base + EIGHT == shards)(lambda: send_chief(shards - 1, 0))
        for k in reversed(range(EIGHT)):
            for g in reversed(range(2, groups)):
                send_chief(base + k, g)
        each(EIGHT, shards, lambda k: [send_chief(row(k), g) for g in range(groups)])

    @pl.when(aide)
    def _():
        own_slim().wait()
        some(slim_in, 2 * shards - 1, slim_sems).wait_recv()
        for g in range(2):
            far_out[pl.ds(g * SPAN, SPAN)] = total(slim_in, g * shards, shards)
        for j in reversed(range(SPAN)):
            for g in range(2):
                owner = base + lax.div(step, 2) * SPAN + j

                @pl.when(jnp.logical_or(owner != d, g != 1))
                def _():
                    send_far(g * SPAN + j, owner, e - 1 + g)

    relay_whole = some(relay_in, groups - 1, relay_sems)

    some(relay_in, groups - 2, relay_sems).wait_recv()
    rows = lax.broadcasted_iota(jnp.int32, (blocks, block), 0)
    placed = [jnp.zeros((blocks, block), jnp.float32) for _ in range(3)]
    for k in range(groups):
        frm = lax.rem(e - k + groups, groups)
        for c in range(q):
            here = rows == place_s[0, frm * q + c]
            for i in range(3):
                row = relay_out[0, i, c : c + 1, :] if k == 0 else relay_in[k - 1, i, c : c + 1, :]
                placed[i] = jnp.where(here, jnp.broadcast_to(row, (blocks, block)), placed[i])
    for i in range(3):
        state_out[i + 1] = placed[i]

    keeps = both(aide, step == 0)

    @pl.when(second)
    def _():
        state_out[0] = far_out[EIGHT + 2]

    @pl.when(keeps)
    def _():
        state_out[0] = far_out[SPAN]

    @pl.when(no(jnp.logical_or(second, keeps)))
    def _():
        some(far_in, 1, far_sems).wait_recv()
        state_out[0] = far_in[0]

    relay_whole.wait_send()

    @pl.when(first)
    def _():
        if eights > 1:
            @pl.when(second)
            def _():
                some(whole_in, eights - 1, grad_sems).wait_send()

        @pl.when(no(second))
        def _():
            some(whole_in, eights, grad_sems).wait_send()

    @pl.when(later)
    def _():
        @pl.when(both(last, odd == 0))
        def _():
            some(wide_in, eights, wide_sems).wait_send()

        @pl.when(aide)
        def _():
            some(slim_in, 2 * eights - 1, slim_sems).wait_send()

        @pl.when(no(aide))
        def _():
            some(slim_in, 2 * eights, slim_sems).wait_send()

        second_in[...] = jnp.zeros_like(second_in)

    if eights > 1:
        @pl.when(second)
        def _():
            some(second_in, eights - 1, second_sems).wait_recv()

        @pl.when(chief)
        def _():
            some(square_in, eights - 1, square_sems).wait_recv()

    @pl.when(both(first, no(jnp.logical_or(chief, second))))
    def _():
        some(second_in, eights, second_sems).wait_recv()

    @pl.when(no(chief))
    def _():
        some(square_in, eights, square_sems).wait_recv()

    lanes_out[...] = jnp.sum(square_in[...], axis=0) + jnp.sum(second_in[...], axis=0)

    @pl.when(jnp.logical_or(jnp.logical_or(chief, second), aide))
    def _():
        @pl.when(keeps)
        def _():
            some(far_out, 2 * SPAN - 1, far_sems).wait_send()

        @pl.when(both(aide, step == 2))
        def _():
            some(far_out, 2 * SPAN, far_sems).wait_send()

        @pl.when(second)
        def _():
            some(square_all, 2 * shards - 1, second_sems).wait_send()
            some(far_out, 2 * EIGHT - 1, far_sems).wait_send()

        @pl.when(chief)
        def _():
            some(square_all, shards * groups - 1, square_sems).wait_send()


def update(count, state, lanes, master_out, mc_out, ms_out, vc_out, vs_out):
    gradient, master, moment_one, moment_two = (state[i] for i in range(4))
    blocks, block = gradient.shape

    total_squares = jnp.sum(lanes[...], axis=1, keepdims=True)
    root_mean = jnp.sqrt(total_squares / count + NORM_EPS)
    clip_factor = jnp.minimum(1.0, CLIP_RMS / root_mean)

    clipped = clip_factor * gradient
    m_next = BETA_ONE * moment_one + (1.0 - BETA_ONE) * clipped
    v_next = BETA_TWO * moment_two + (1.0 - BETA_TWO) * clipped * clipped
    bias_one = 1.0 - BETA_ONE**STEP
    bias_two = 1.0 - BETA_TWO**STEP
    m_mag = jnp.max(jnp.abs(m_next), axis=1, keepdims=True) + QUANT_EPS
    v_mag = jnp.max(jnp.abs(v_next), axis=1, keepdims=True) + QUANT_EPS
    step = m_next / bias_one / (jnp.sqrt(v_next / bias_two) + ADAM_EPS)
    master_out[...] = master - LEARN_RATE * (step + DECAY_RATE * master)
    mc_out[...] = (m_next / m_mag).astype(jnp.bfloat16)
    vc_out[...] = (v_next / v_mag).astype(jnp.bfloat16)
    rows = lax.broadcasted_iota(jnp.int32, (blocks, block), 0)
    diagonal = rows == lax.broadcasted_iota(jnp.int32, (blocks, block), 1)
    ms_out[...] = jnp.sum(jnp.where(diagonal, m_mag, 0.0), axis=0, keepdims=True)[:, :blocks]
    vs_out[...] = jnp.sum(jnp.where(diagonal, v_mag, 0.0), axis=0, keepdims=True)[:, :blocks]


def body(shards, groups, master_old, m_codes, m_scale, v_codes, v_scale, grad_parts, send_order, recv_place):
    blocks, block = master_old.shape[2:]
    eights = shards // EIGHT
    f32, bf16 = jnp.float32, jnp.bfloat16
    wide = (blocks, block)
    anywhere = pl.BlockSpec(memory_space=pl.ANY)
    vmem = pl.BlockSpec(memory_space=pltpu.VMEM)
    state, lanes = pl.pallas_call(
        functools.partial(kernel, shards, groups),
        out_shape=(pltpu.VMEM((4, blocks, block), f32), pltpu.VMEM((1, block), f32)),
        in_specs=[anywhere] * 8,
        out_specs=(vmem, vmem),
        scratch_shapes=[
            pltpu.VMEM(wide, f32),
            pltpu.VMEM(wide, bf16),
            pltpu.VMEM(wide, bf16),
            pltpu.VMEM(wide, f32),
            pltpu.VMEM(wide, f32),
            pltpu.SMEM((1, blocks), f32),
            pltpu.SMEM((1, blocks), f32),
            pltpu.SMEM((1, blocks), jnp.int32),
            pltpu.SMEM((1, blocks), jnp.int32),
            pltpu.VMEM((groups, 3, blocks // groups, block), f32),
            pltpu.VMEM((groups - 1, 3, blocks // groups, block), f32),
            pltpu.VMEM((2 * shards, EIGHT, blocks, block), bf16),
            pltpu.VMEM(((groups - 2) * shards, EIGHT, blocks, block), bf16),
            pltpu.VMEM((2 * shards, SPAN, blocks, block), bf16),
            pltpu.VMEM((2 * EIGHT, blocks, block), f32),
            pltpu.VMEM((1, blocks, block), f32),
            pltpu.VMEM((groups - 2, EIGHT, blocks, block), f32),
            pltpu.VMEM((1, block), f32),
            pltpu.VMEM((1, block), f32),
            pltpu.VMEM((eights, 1, block), f32),
            pltpu.VMEM((eights, 1, block), f32),
            pltpu.VMEM((shards * groups - 1, 1, block), f32),
            pltpu.SemaphoreType.DMA((8,)),
            pltpu.SemaphoreType.DMA((3,)),
            pltpu.SemaphoreType.DMA((2,)),
            pltpu.SemaphoreType.DMA((4,)),
            pltpu.SemaphoreType.DMA((4,)),
            pltpu.SemaphoreType.DMA((2,)),
            pltpu.SemaphoreType.DMA((2,)),
            pltpu.SemaphoreType.DMA((2,)),
        ],
        compiler_params=pltpu.CompilerParams(collective_id=0, has_side_effects=True),
    )(
        master_old.reshape(wide), m_codes.reshape(wide), m_scale.reshape(1, blocks),
        v_codes.reshape(wide), v_scale.reshape(1, blocks),
        grad_parts.reshape(eights, EIGHT, blocks, block),
        send_order.reshape(1, blocks), recv_place.reshape(1, blocks),
    )
    master_new, mc, ms, vc, vs = pl.pallas_call(
        functools.partial(update, shards * groups * blocks * block),
        out_shape=(
            jax.ShapeDtypeStruct(wide, f32),
            jax.ShapeDtypeStruct(wide, bf16),
            jax.ShapeDtypeStruct((1, blocks), f32),
            jax.ShapeDtypeStruct(wide, bf16),
            jax.ShapeDtypeStruct((1, blocks), f32),
        ),
        in_specs=[vmem, vmem],
        out_specs=(vmem,) * 5,
    )(
        pltpu.with_memory_space_constraint(state, pltpu.VMEM),
        pltpu.with_memory_space_constraint(lanes, pltpu.VMEM))
    return master_new[None], mc[None], ms, vc[None], vs


def solution(mesh):
    rows = P("dp", "expert", None, None)
    flat = P("dp", "expert", None)
    return jax.shard_map(
        functools.partial(body, mesh.shape["dp"], mesh.shape["expert"]),
        mesh=mesh,
        in_specs=(rows, rows, flat, rows, flat, rows, flat, flat),
        out_specs=(
            P("expert", "dp", None),
            P("expert", "dp", None),
            P("expert", "dp"),
            P("expert", "dp", None),
            P("expert", "dp"),
        ),
        check_vma=False,
    )
```

```python
import functools

import jax
import jax.numpy as jnp
from jax import lax
from jax.experimental import pallas as pl
from jax.experimental.pallas import tpu as pltpu
from jax.sharding import PartitionSpec as P

STEP = 200

BETA_ONE = 0.9
BETA_TWO = 0.999
ADAM_EPS = 1e-08
LEARN_RATE = 0.05
DECAY_RATE = 0.1
CLIP_RMS = 1.0
QUANT_EPS = 1e-06
NORM_EPS = 1e-06

MESH = pl.DeviceIdType.MESH
UNROLL = 40
SUBLANES = 8
EIGHT = 8
SPAN = EIGHT // 2


def each(first, last, step):
    if last - first <= UNROLL:
        for k in range(first, last):
            step(k)
    else:
        lax.fori_loop(first, last, lambda k, c: (step(k), c)[1], 0)


def kernel(
    shards, groups,
    master_in, mc_in, ms_in, vc_in, vs_in, grads_in, order_in, place_in,
    state_out, lanes_out,
    master_v, mc_v, vc_v, m_wide, v_wide,
    ms_s, vs_s, order_s, place_s,
    relay_out, relay_in, whole_in, wide_in, slim_in, far_out, far_in,
    wide_sum, square_out, mixed_out, square_in, second_in, square_all,
    in_sems, grad_sems, slim_sems, wide_sems, relay_sems, far_sems, square_sems, second_sems,
):
    d = lax.axis_index("dp")
    e = lax.axis_index("expert")
    blocks, block = master_v.shape
    q = blocks // groups
    eights = shards // EIGHT
    odd = lax.rem(e, 2)
    pair = lax.div(e, 2)
    eight = lax.div(d, EIGHT) if eights > 1 else 0
    step = lax.rem(d, EIGHT) if eights > 1 else d
    base = EIGHT * eight
    both = jnp.logical_and
    no = jnp.logical_not
    first = e < 2
    later = e >= 2
    chief = both(e == 1, step == 0)
    second = both(e == 1, step == 2)
    aide = both(both(odd == 1, later), jnp.logical_or(step == 0, step == 2))
    last = d == shards - 1
    leader = jnp.where(last, 1, 3)

    barrier = pltpu.get_barrier_semaphore()

    def greet(shard, group):
        pl.semaphore_signal(barrier, inc=1, device_id=(shard, group), device_id_type=MESH)

    @pl.when(e != 2)
    def _():
        @pl.when(chief)
        def _():
            each(0, shards, lambda k: [greet(lax.rem(d + k, shards), g) for g in range(2, groups)])

        @pl.when(jnp.logical_or(second, aide))
        def _():
            greet(d, e - 1)
            each(1, shards, lambda k: [greet(lax.rem(d + k, shards), e - g) for g in range(2)])

        @pl.when(e == 0)
        def _():
            greet(d, leader)

        @pl.when(e != 0)
        def _():
            greet(d, 2)

    greeters = (
        jnp.where(first, eights, 3 * eights)
        - jnp.logical_or(second, aide).astype(jnp.int32)
        + jnp.where(e == 2, groups - 2, jnp.where(e == leader, 1, 0)))

    @pl.when(greeters > 0)
    def _():
        pl.semaphore_wait(barrier, greeters)

    source = odd * shards + d

    def send(src, dst, shard, group, sems, arrives=1):
        @pl.when(jnp.logical_or(d != shard, e != group))
        def _():
            pltpu.make_async_remote_copy(
                src_ref=src, dst_ref=dst, send_sem=sems.at[0], recv_sem=sems.at[arrives],
                device_id=(shard, group), device_id_type=MESH).start()

    def send_first(i):
        send(grads_in.at[i], whole_in.at[source], EIGHT * i + 2, 1, grad_sems, jnp.where(last, 2, 1))

    arrival = jnp.where(last, 3 - odd, 1)

    def send_wide(i):
        pltpu.make_async_remote_copy(
            src_ref=grads_in.at[i], dst_ref=wide_in.at[(e - 2) * shards + d],
            send_sem=wide_sems.at[0], recv_sem=wide_sems.at[arrival],
            device_id=(EIGHT * i, 1), device_id_type=MESH).start()

    def send_slim(i):
        send(grads_in.at[i, pl.ds(0, SPAN)], slim_in.at[source], EIGHT * i, 2 * pair + 1, slim_sems)
        send(grads_in.at[i, pl.ds(SPAN, SPAN)], slim_in.at[source], EIGHT * i + 2, 2 * pair + 1, slim_sems)

    @pl.when(later)
    def _():
        each(0, eights, send_wide)

    @pl.when(first)
    def _():
        each(0, eights, send_first)

    def own_first():
        return pltpu.make_async_copy(grads_in.at[eight], whole_in.at[shards + d], in_sems.at[7])

    def own_slim():
        return pltpu.make_async_copy(
            grads_in.at[eight, pl.ds(lax.div(step, 2) * SPAN, SPAN)], slim_in.at[shards + d], in_sems.at[7])

    @pl.when(second)
    def _():
        own_first().start()

    @pl.when(aide)
    def _():
        own_slim().start()

    loads = [
        pltpu.make_async_copy(src, dst, in_sems.at[i])
        for i, (src, dst) in enumerate((
            (order_in, order_s), (ms_in, ms_s), (vs_in, vs_s),
            (mc_in, mc_v), (vc_in, vc_v), (master_in, master_v), (place_in, place_s),
        ))
    ]
    for load in loads:
        load.start()
    for load in loads:
        load.wait()
    m_wide[...] = mc_v[...].astype(jnp.float32)
    v_wide[...] = vc_v[...].astype(jnp.float32)

    def relay_copy(k, sem):
        return pltpu.make_async_remote_copy(
            src_ref=relay_out.at[k], dst_ref=relay_in.at[k - 1],
            send_sem=relay_sems.at[0], recv_sem=relay_sems.at[sem],
            device_id=(d, lax.rem(e + k, groups)), device_id_type=MESH)

    for k in range(groups):
        to = lax.rem(e + k, groups)
        for c in range(q):
            row = order_s[0, to * q + c]
            relay_out[k, 0, c : c + 1, :] = master_v[pl.ds(row, 1), :]
            relay_out[k, 1, c : c + 1, :] = m_wide[pl.ds(row, 1), :] * ms_s[0, row]
            relay_out[k, 2, c : c + 1, :] = v_wide[pl.ds(row, 1), :] * vs_s[0, row]

    def some(ref, count, sems):
        part = ref.at[pl.ds(0, count)]
        return pltpu.make_async_remote_copy(
            src_ref=part, dst_ref=part, send_sem=sems.at[0], recv_sem=sems.at[1],
            device_id=(d, lax.rem(e + 1, groups)), device_id_type=MESH)

    to_leader = lax.rem(leader - 2 + groups, groups)

    @pl.when(e == 2)
    def _():
        relay_copy(to_leader, 3).start()

    @pl.when(both(later, no(both(last, odd == 0))))
    def _():
        some(wide_in, eights, wide_sems).wait_send()

    @pl.when(later)
    def _():
        each(0, eights, send_slim)

    @pl.when(e == leader)
    def _():
        relay_copy(to_leader, 3).wait_recv()
        for k in range(1, groups):
            relay_copy(k, 2).start()

    @pl.when(e != leader)
    def _():
        relay_copy(1, 2).wait_recv()
        for k in range(1, groups):
            @pl.when(jnp.logical_or(e != 2, k != to_leader))
            def _():
                relay_copy(k, 1).start()

    def total(arrived, begin, count):
        if count <= UNROLL:
            gradient = arrived[begin].astype(jnp.float32)
            for k in range(1, count):
                gradient = gradient + arrived[begin + k].astype(jnp.float32)
            return gradient
        return lax.fori_loop(
            0, count, lambda k, g: g + arrived[begin + k].astype(jnp.float32),
            jnp.zeros(arrived.shape[1:], jnp.float32))

    def fold(gradient):
        return jnp.sum((gradient * gradient).reshape(-1, SUBLANES, block), axis=0)

    def send_square(shard, group, out, to, sems):
        pltpu.make_async_remote_copy(
            src_ref=out, dst_ref=to, send_sem=sems.at[0], recv_sem=sems.at[1],
            device_id=(shard, group), device_id_type=MESH).start()

    def send_second(shard, group):
        send_square(shard, group, square_out, second_in.at[eight], second_sems)

    def send_chief(shard, group):
        send_square(shard, group, square_out if group < 2 else mixed_out, square_in.at[eight], square_sems)

    def send_far(at, shard, group):
        pltpu.make_async_remote_copy(
            src_ref=far_out.at[at], dst_ref=far_in.at[0],
            send_sem=far_sems.at[0], recv_sem=far_sems.at[1],
            device_id=(shard, group), device_id_type=MESH).start()

    def row(k):
        return lax.rem(base + k, shards)

    @pl.when(second)
    def _():
        own_first().wait()
        some(whole_in, 2 * (shards - 1) - 1, grad_sems).wait_recv()
        for g in range(2):
            far_out[pl.ds(g * EIGHT, EIGHT)] = total(whole_in, g * shards, shards - 1)
        pltpu.make_async_remote_copy(
            src_ref=whole_in.at[pl.ds(0, 2)], dst_ref=whole_in.at[pl.ds(0, 2)],
            send_sem=grad_sems.at[0], recv_sem=grad_sems.at[2],
            device_id=(base, 0), device_id_type=MESH).wait_recv()
        squares = jnp.zeros((SUBLANES, block), jnp.float32)
        for g in range(2):
            gradient = far_out[pl.ds(g * EIGHT, EIGHT)] + whole_in[g * shards + shards - 1].astype(jnp.float32)
            squares = squares + fold(gradient)
            far_out[pl.ds(g * EIGHT, EIGHT)] = gradient
        squares = jnp.sum(squares, axis=0, keepdims=True)
        square_out[...] = squares
        second_in[eight] = squares
        send_second(base, 1)
        send_second(base, 0)
        for k in range(1, EIGHT):
            for g in range(2):
                if k != 2 or g != 1:
                    send_second(base + k, g)
        send_far(0, base, 0)
        send_far(EIGHT, base, 1)
        for k in range(1, EIGHT):
            for g in range(2):
                if k != 2 or g != 1:
                    send_far(g * EIGHT + k, base + k, g)
        each(EIGHT, shards, lambda k: [send_second(row(k), g) for g in range(2)])

    @pl.when(chief)
    def _():
        some(wide_in, (groups - 2) * (shards - 1), wide_sems).wait_recv()
        for g in range(groups - 2):
            wide_sum[g] = total(wide_in, g * shards, shards - 1)
        squares = jnp.zeros((SUBLANES, block), jnp.float32)
        half = wide_in.at[pl.ds(0, groups // 2 - 1)]
        for parity in (1, 0):
            pltpu.make_async_remote_copy(
                src_ref=half, dst_ref=half, send_sem=wide_sems.at[0], recv_sem=wide_sems.at[3 - parity],
                device_id=(base, 0), device_id_type=MESH).wait_recv()
            for g in range(parity, groups - 2, 2):
                squares = squares + fold(wide_sum[g] + wide_in[g * shards + shards - 1].astype(jnp.float32))
        squares = jnp.sum(squares, axis=0, keepdims=True)
        square_out[...] = squares
        square_in[eight] = squares
        send_chief(base, 0)
        for k in reversed(range(1, EIGHT)):
            send_chief(base + k, 1)
            pl.when(base + k != shards - 1)(lambda: send_chief(base + k, 0))
        some(second_in, eights, second_sems).wait_recv()
        mixed_out[...] = square_out[...] + second_in[eight]
        pl.when(base + EIGHT == shards)(lambda: send_chief(shards - 1, 0))
        for k in reversed(range(EIGHT)):
            for g in reversed(range(2, groups)):
                send_chief(base + k, g)
        each(EIGHT, shards, lambda k: [send_chief(row(k), g) for g in range(groups)])

    @pl.when(aide)
    def _():
        own_slim().wait()
        some(slim_in, 2 * shards - 1, slim_sems).wait_recv()
        for g in range(2):
            far_out[pl.ds(g * SPAN, SPAN)] = total(slim_in, g * shards, shards)
        for j in reversed(range(SPAN)):
            for g in range(2):
                owner = base + lax.div(step, 2) * SPAN + j

                @pl.when(jnp.logical_or(owner != d, g != 1))
                def _():
                    send_far(g * SPAN + j, owner, e - 1 + g)

    relay_whole = some(relay_in, groups - 1, relay_sems)

    some(relay_in, groups - 2, relay_sems).wait_recv()
    rows = lax.broadcasted_iota(jnp.int32, (blocks, block), 0)
    placed = [jnp.zeros((blocks, block), jnp.float32) for _ in range(3)]
    for k in range(groups):
        frm = lax.rem(e - k + groups, groups)
        for c in range(q):
            here = rows == place_s[0, frm * q + c]
            for i in range(3):
                row = relay_out[0, i, c : c + 1, :] if k == 0 else relay_in[k - 1, i, c : c + 1, :]
                placed[i] = jnp.where(here, jnp.broadcast_to(row, (blocks, block)), placed[i])
    for i in range(3):
        state_out[i + 1] = placed[i]

    keeps = both(aide, step == 0)

    @pl.when(second)
    def _():
        state_out[0] = far_out[EIGHT + 2]

    @pl.when(keeps)
    def _():
        state_out[0] = far_out[SPAN]

    @pl.when(no(jnp.logical_or(second, keeps)))
    def _():
        some(far_in, 1, far_sems).wait_recv()
        state_out[0] = far_in[0]

    relay_whole.wait_send()

    @pl.when(first)
    def _():
        if eights > 1:
            @pl.when(second)
            def _():
                some(whole_in, eights - 1, grad_sems).wait_send()

        @pl.when(no(second))
        def _():
            some(whole_in, eights, grad_sems).wait_send()

    @pl.when(later)
    def _():
        @pl.when(both(last, odd == 0))
        def _():
            some(wide_in, eights, wide_sems).wait_send()

        @pl.when(aide)
        def _():
            some(slim_in, 2 * eights - 1, slim_sems).wait_send()

        @pl.when(no(aide))
        def _():
            some(slim_in, 2 * eights, slim_sems).wait_send()

        second_in[...] = jnp.zeros_like(second_in)

    if eights > 1:
        @pl.when(second)
        def _():
            some(second_in, eights - 1, second_sems).wait_recv()

        @pl.when(chief)
        def _():
            some(square_in, eights - 1, square_sems).wait_recv()

    @pl.when(both(first, no(jnp.logical_or(chief, second))))
    def _():
        some(second_in, eights, second_sems).wait_recv()

    @pl.when(no(chief))
    def _():
        some(square_in, eights, square_sems).wait_recv()

    lanes_out[...] = jnp.sum(square_in[...], axis=0) + jnp.sum(second_in[...], axis=0)

    @pl.when(jnp.logical_or(jnp.logical_or(chief, second), aide))
    def _():
        @pl.when(keeps)
        def _():
            some(far_out, 2 * SPAN - 1, far_sems).wait_send()

        @pl.when(both(aide, step == 2))
        def _():
            some(far_out, 2 * SPAN, far_sems).wait_send()

        @pl.when(second)
        def _():
            some(square_all, 2 * shards - 1, second_sems).wait_send()
            some(far_out, 2 * EIGHT - 1, far_sems).wait_send()

        @pl.when(chief)
        def _():
            some(square_all, shards * groups - 1, square_sems).wait_send()


def update(count, state, lanes, master_out, mc_out, ms_out, vc_out, vs_out):
    gradient, master, moment_one, moment_two = (state[i] for i in range(4))
    blocks, block = gradient.shape

    total_squares = jnp.sum(lanes[...], axis=1, keepdims=True)
    root_mean = jnp.sqrt(total_squares / count + NORM_EPS)
    clip_factor = jnp.minimum(1.0, CLIP_RMS / root_mean)

    clipped = clip_factor * gradient
    m_next = BETA_ONE * moment_one + (1.0 - BETA_ONE) * clipped
    v_next = BETA_TWO * moment_two + (1.0 - BETA_TWO) * clipped * clipped
    bias_one = 1.0 - BETA_ONE**STEP
    bias_two = 1.0 - BETA_TWO**STEP
    m_mag = jnp.max(jnp.abs(m_next), axis=1, keepdims=True) + QUANT_EPS
    v_mag = jnp.max(jnp.abs(v_next), axis=1, keepdims=True) + QUANT_EPS
    step = m_next / bias_one / (jnp.sqrt(v_next / bias_two) + ADAM_EPS)
    master_out[...] = master - LEARN_RATE * (step + DECAY_RATE * master)
    mc_out[...] = (m_next / m_mag).astype(jnp.bfloat16)
    vc_out[...] = (v_next / v_mag).astype(jnp.bfloat16)
    rows = lax.broadcasted_iota(jnp.int32, (blocks, block), 0)
    diagonal = rows == lax.broadcasted_iota(jnp.int32, (blocks, block), 1)
    ms_out[...] = jnp.sum(jnp.where(diagonal, m_mag, 0.0), axis=0, keepdims=True)[:, :blocks]
    vs_out[...] = jnp.sum(jnp.where(diagonal, v_mag, 0.0), axis=0, keepdims=True)[:, :blocks]


def body(shards, groups, master_old, m_codes, m_scale, v_codes, v_scale, grad_parts, send_order, recv_place):
    blocks, block = master_old.shape[2:]
    eights = shards // EIGHT
    f32, bf16 = jnp.float32, jnp.bfloat16
    wide = (blocks, block)
    anywhere = pl.BlockSpec(memory_space=pl.ANY)
    vmem = pl.BlockSpec(memory_space=pltpu.VMEM)
    state, lanes = pl.pallas_call(
        functools.partial(kernel, shards, groups),
        out_shape=(pltpu.VMEM((4, blocks, block), f32), pltpu.VMEM((1, block), f32)),
        in_specs=[anywhere] * 8,
        out_specs=(vmem, vmem),
        scratch_shapes=[
            pltpu.VMEM(wide, f32),
            pltpu.VMEM(wide, bf16),
            pltpu.VMEM(wide, bf16),
            pltpu.VMEM(wide, f32),
            pltpu.VMEM(wide, f32),
            pltpu.SMEM((1, blocks), f32),
            pltpu.SMEM((1, blocks), f32),
            pltpu.SMEM((1, blocks), jnp.int32),
            pltpu.SMEM((1, blocks), jnp.int32),
            pltpu.VMEM((groups, 3, blocks // groups, block), f32),
            pltpu.VMEM((groups - 1, 3, blocks // groups, block), f32),
            pltpu.VMEM((2 * shards, EIGHT, blocks, block), bf16),
            pltpu.VMEM(((groups - 2) * shards, EIGHT, blocks, block), bf16),
            pltpu.VMEM((2 * shards, SPAN, blocks, block), bf16),
            pltpu.VMEM((2 * EIGHT, blocks, block), f32),
            pltpu.VMEM((1, blocks, block), f32),
            pltpu.VMEM((groups - 2, EIGHT, blocks, block), f32),
            pltpu.VMEM((1, block), f32),
            pltpu.VMEM((1, block), f32),
            pltpu.VMEM((eights, 1, block), f32),
            pltpu.VMEM((eights, 1, block), f32),
            pltpu.VMEM((shards * groups - 1, 1, block), f32),
            pltpu.SemaphoreType.DMA((8,)),
            pltpu.SemaphoreType.DMA((3,)),
            pltpu.SemaphoreType.DMA((2,)),
            pltpu.SemaphoreType.DMA((4,)),
            pltpu.SemaphoreType.DMA((4,)),
            pltpu.SemaphoreType.DMA((2,)),
            pltpu.SemaphoreType.DMA((2,)),
            pltpu.SemaphoreType.DMA((2,)),
        ],
        compiler_params=pltpu.CompilerParams(collective_id=0, has_side_effects=True),
    )(
        master_old.reshape(wide), m_codes.reshape(wide), m_scale.reshape(1, blocks),
        v_codes.reshape(wide), v_scale.reshape(1, blocks),
        grad_parts.reshape(eights, EIGHT, blocks, block),
        send_order.reshape(1, blocks), recv_place.reshape(1, blocks),
    )
    master_new, mc, ms, vc, vs = pl.pallas_call(
        functools.partial(update, shards * groups * blocks * block),
        out_shape=(
            jax.ShapeDtypeStruct(wide, f32),
            jax.ShapeDtypeStruct(wide, bf16),
            jax.ShapeDtypeStruct((1, blocks), f32),
            jax.ShapeDtypeStruct(wide, bf16),
            jax.ShapeDtypeStruct((1, blocks), f32),
        ),
        in_specs=[vmem, vmem],
        out_specs=(vmem,) * 5,
    )(
        pltpu.with_memory_space_constraint(state, pltpu.VMEM),
        pltpu.with_memory_space_constraint(lanes, pltpu.VMEM))
    return master_new[None], mc[None], ms, vc[None], vs


def solution(mesh):
    rows = P("dp", "expert", None, None)
    flat = P("dp", "expert", None)
    return jax.shard_map(
        functools.partial(body, mesh.shape["dp"], mesh.shape["expert"]),
        mesh=mesh,
        in_specs=(rows, rows, flat, rows, flat, rows, flat, flat),
        out_specs=(
            P("expert", "dp", None),
            P("expert", "dp", None),
            P("expert", "dp"),
            P("expert", "dp", None),
            P("expert", "dp"),
        ),
        check_vma=False,
    )
```
